512 devices in a mesh: tex: 64 (over x, z_lo, core), view: 8 (over y, z_hi).
Axes of the slice: x: 4, y: 4, z: 16 (z_hi: 2, z_lo: 8; z = z_hi * 8 + z_lo), core: 2. Of those that a mesh axis runs over, the one named last changes fastest.
Arguments:
- measured: bfloat16 [1536, 160, 151], P('tex', 'view'), may hold values from -6 to 6
- view_mask: int32 [160], P('view'), may hold values from 0 to 1, as said below
- tex_factor: float32 [1536, 256], P('tex'), may hold values from -6 to 6
- view_factor: float32 [160, 64], P('view'), as said below
- light_factor: bfloat16 [151, 64], replicated, as said below
- core_tensor: float32 [256, 64, 64], P('tex', 'view'), may hold values from -6 to 6
Outputs:
- tex_updated: float32 [1536, 256], P('tex')
- view_updated: float32 [160, 64], P('view')
- core_updated: float32 [256, 64, 64], P('tex', 'view')
The draws below stay inside these ranges and needn't reach their ends.
Inputs may be any that keep to these rules, and one draw needn't show every extreme that they name: `view_mask`: exactly 151 of the 160 entries are 1. `view_factor`: entries of order one. `light_factor`: entries of order one.
All inputs are finite; a program needn't handle non-finite values.
Results may differ from the reference program's by a relative error of at most 0.014.
Values may be sent and summed in bfloat16 or wider, within the bound.
No kernel may reach another device: no remote copies, remote signals or barrier semaphores. Data moves between devices by JAX's collectives and lax.ppermute only.
A program may use at most 64 MiB of HBM per device.

```python
import math
import jax
import jax.numpy as jnp
from jax import lax

RT = 256
RV = 64
RL = 64
VIEWS = 160
VALID = 151
L = 151
TD = 24
STEPS = 1
TEXELS = 1536
N_VIEW = 8


def spread_columns(key, rows, cols):
    sample = jax.random.normal(key, (rows, cols), jnp.float32)
    matrix = sample / jnp.linalg.norm(sample)
    for sweep in range(30):
        gram_matrix = jnp.dot(matrix.T, matrix, precision=lax.Precision.HIGHEST)
        matrix = 1.5 * matrix - 0.5 * jnp.dot(matrix, gram_matrix, precision=lax.Precision.HIGHEST)
    return matrix * math.sqrt(rows)


def draw_view_mask(key, part):
    order = jax.random.permutation(jax.random.fold_in(key, 11), VIEWS)
    return (order < VALID).astype(jnp.int32)


def draw_view_factor(key, part):
    return spread_columns(jax.random.fold_in(key, 23), VIEWS, RV)


def draw_light_factor(key, part):
    return spread_columns(jax.random.fold_in(key, 37), L, RL).astype(jnp.bfloat16)


def shard_levels(own_key, shape, pieces, smallest, high):
    loudness, own = 1.0, jax.random.fold_in(own_key, 6)
    for position, shards_of in pieces:
        heights = jnp.exp(jax.random.uniform(jax.random.fold_in(own, position), (shards_of,), jnp.float32, smallest / len(pieces), high / len(pieces)))
        loudness = loudness * jnp.repeat(heights, shape[position] // shards_of).reshape([-1 if axis == position else 1 for axis in range(len(shape))])
    return loudness


def noise(stream_key, shape, scale, bound, split=(), held_as=jnp.bfloat16):
    factor_of = shard_levels(stream_key, shape, split, -0.22, 0.18) if split else 1.0
    values = jax.random.normal(stream_key, shape, jnp.float32) * scale * factor_of
    return jnp.minimum(jnp.maximum(values, -bound), bound).astype(held_as)


def setup_inputs(seed: int = 0) -> dict:
    arg_keys = jax.random.split(jax.random.key(seed), 7)
    return {
        "measured": noise(arg_keys[0], (TEXELS, VIEWS, L), 1.0, 6.0, ((0, 64), (1, 8))),
        "view_mask": draw_view_mask(jax.random.fold_in(arg_keys[6], 71), 0),
        "tex_factor": noise(arg_keys[2], (TEXELS, RT), 1.0, 6.0, ((0, 64),), jnp.float32),
        "view_factor": draw_view_factor(jax.random.fold_in(arg_keys[6], 71), 0),
        "light_factor": draw_light_factor(jax.random.fold_in(arg_keys[6], 71), 0),
        "core_tensor": noise(arg_keys[5], (RT, RV, RL), 1.0, 6.0, ((0, 64), (1, 8)), jnp.float32),
    }


def round_trip(values):
    return lax.optimization_barrier(values.astype(jnp.bfloat16)).astype(jnp.float32)

def reference(measured, view_mask, tex_factor, view_factor, light_factor, core_tensor):
    scaling = (RT * RV * RL) ** (-0.5)
    rate_tex = RT / (VALID * L)
    rate_view = RV / (TEXELS * L)
    rate_core = RT * RV * RL / (TEXELS * VALID * L)
    weights = view_mask.astype(jnp.float32)[None, :, None]
    light_full = light_factor.astype(jnp.float32)
    blocks = measured.reshape(TEXELS // TD, TD, VIEWS, L)
    tex_now = tex_factor
    view_now = view_factor
    core_now = core_tensor
    for iteration in range(STEPS):
        tex_bf = tex_now.astype(jnp.bfloat16)
        view_bf = view_now.astype(jnp.bfloat16)
        core_bf = core_now.astype(jnp.bfloat16)
        core_flat = core_bf.reshape(RT, RV * RL)
        projected = jnp.dot(tex_bf.astype(jnp.float32), core_flat.astype(jnp.float32), preferred_element_type=jnp.float32).astype(jnp.bfloat16)
        proj_blocks = projected.reshape(TEXELS // TD, TD, RV, RL)
        view_full = view_bf.astype(jnp.float32)
        view_groups = view_full.reshape(N_VIEW, VIEWS // N_VIEW, RV)

        def per_block(total, inputs):
            sample, proj_block = inputs
            proj_full = proj_block.astype(jnp.float32)
            mixed = round_trip(jnp.einsum('vb,tbc->tvc', view_full, proj_full))
            approx = jnp.einsum('tvc,lc->tvl', mixed, light_full)
            resid = round_trip(weights * (scaling * approx - sample.astype(jnp.float32)))
            back = round_trip(jnp.einsum('tvl,lc->tvc', resid, light_full))
            grad_part = scaling * jnp.einsum('tvc,tbc->vb', back, proj_full)
            grouped = back.reshape(TD, N_VIEW, VIEWS // N_VIEW, RL)
            partials = round_trip(jnp.einsum('gvb,tgvc->tgbc', view_groups, grouped))
            return (total + grad_part, jnp.sum(partials, axis=1).astype(jnp.bfloat16))
        grad_view, summed = lax.scan(per_block, jnp.zeros((VIEWS, RV), jnp.float32), (blocks, proj_blocks))
        summed_flat = summed.reshape(TEXELS, RV * RL)
        grad_tex = scaling * lax.dot_general(summed_flat.astype(jnp.float32), core_flat.astype(jnp.float32), (((1,), (1,)), ((), ())), preferred_element_type=jnp.float32)
        grad_core = scaling * lax.dot_general(tex_bf.astype(jnp.float32), summed_flat.astype(jnp.float32), (((0,), (0,)), ((), ())), preferred_element_type=jnp.float32)
        tex_now = tex_now - rate_tex * grad_tex
        view_now = view_now - rate_view * grad_view
        core_now = core_now - rate_core * grad_core.reshape(RT, RV, RL)
    return (tex_now, view_now, core_now)
```

```python
import jax
import jax.numpy as jnp
from jax import lax
from jax.sharding import PartitionSpec as P

RT = 256
RV = 64
RL = 64
VALID = 151
L = 151

F32 = jnp.float32
BF16 = jnp.bfloat16


def gather_blocks(x, axis):
    count = lax.axis_size(axis)
    return lax.all_to_all(
        jnp.broadcast_to(x[None], (count,) + x.shape), axis, 0, 0, tiled=True
    )


def sum_blocks(x):
    return jnp.sum(x.astype(F32), axis=0)


def per_device(measured, view_mask, tex_factor, view_factor, light_factor, core_tensor):
    tex_count = lax.axis_size("tex")
    view_count = lax.axis_size("view")
    tex_rows, views = measured.shape[:2]
    core_rows, band = core_tensor.shape[:2]
    width = band * RL
    texels_all = tex_rows * tex_count
    scaling = (RT * RV * RL) ** (-0.5)
    rate_tex = RT / (VALID * L)
    rate_view = RV / (texels_all * L)
    rate_core = RT * RV * RL / (texels_all * VALID * L)
    weights = view_mask.astype(F32)[:, None, None]
    tex_bf = tex_factor.astype(BF16)
    view_bf = view_factor.astype(BF16)
    core_bf = core_tensor.astype(BF16).reshape(core_rows, width)

    core_band = gather_blocks(core_bf, "tex").reshape(RT, width)
    proj_band = jnp.dot(tex_bf, core_band, preferred_element_type=F32).astype(BF16)
    projected = gather_blocks(proj_band, "view")
    projected = projected.reshape(view_count, tex_rows, band, RL)
    view_bands = view_bf.reshape(views, view_count, band)

    mixed = jnp.einsum(
        "vgb,gtbc->vtc", view_bands, projected, preferred_element_type=F32
    ).astype(BF16)
    approx = jnp.einsum("vtc,lc->vtl", mixed, light_factor, preferred_element_type=F32)
    target = jnp.transpose(measured, (1, 0, 2)).astype(F32)
    resid = (weights * (scaling * approx - target)).astype(BF16)
    back = jnp.einsum("vtl,lc->vtc", resid, light_factor, preferred_element_type=F32).astype(BF16)

    partial_y = jnp.einsum("vgb,vtc->gtbc", view_bands, back, preferred_element_type=F32)
    partial_y = partial_y.astype(BF16).reshape(view_count, tex_rows, width)
    summed = sum_blocks(lax.all_to_all(partial_y, "view", 0, 0, tiled=True)).astype(BF16)

    tex_part = lax.dot_general(
        summed, core_band, (((1,), (1,)), ((), ())), preferred_element_type=F32
    )
    grad_tex = scaling * sum_blocks(gather_blocks(tex_part.astype(BF16), "view"))

    view_part = jnp.einsum("vtc,gtbc->vgb", back, projected, preferred_element_type=F32)
    core_part = lax.dot_general(
        tex_bf, summed, (((0,), (0,)), ((), ())), preferred_element_type=F32
    )
    core_part = core_part.astype(BF16).reshape(tex_count, core_rows * width)
    view_part = view_part.astype(BF16).reshape(1, views * RV)
    view_part = jnp.broadcast_to(view_part, (tex_count, views * RV))
    both = jnp.concatenate([core_part, view_part], axis=1)
    both = sum_blocks(lax.all_to_all(both, "tex", 0, 0, tiled=True))
    grad_core = scaling * both[: core_rows * width].reshape(core_tensor.shape)
    grad_view = scaling * both[core_rows * width :].reshape(view_factor.shape)

    return (
        tex_factor - rate_tex * grad_tex,
        view_factor - rate_view * grad_view,
        core_tensor - rate_core * grad_core,
    )


def solution(mesh):
    return jax.shard_map(
        per_device,
        mesh=mesh,
        in_specs=(
            P("tex", "view", None),
            P("view"),
            P("tex", None),
            P("view", None),
            P(),
            P("tex", "view", None),
        ),
        out_specs=(P("tex", None), P("view", None), P("tex", "view", None)),
        check_vma=False,
    )
```

```python
import jax
import jax.numpy as jnp
from jax import lax
from jax.sharding import Mesh, PartitionSpec as P

RT = 256
RV = 64
RL = 64
VALID = 151
L = 151

F32 = jnp.float32
BF16 = jnp.bfloat16

SIZES = (4, 8, 2, 4, 2)
NAMES = ("x", "zl", "c", "y", "zh")
TEX = ("x", "zl", "c")
VIEW = ("y", "zh")


def exchange(x, axes):
    return lax.all_to_all(x, axes, 0, 0, tiled=True)


def gather_blocks(x, axes):
    count = lax.axis_size(axes)
    return exchange(jnp.broadcast_to(x[None], (count,) + x.shape), axes)


def sum_blocks(x):
    return jnp.sum(x.astype(F32), axis=0)


def column_order():
    i = lax.broadcasted_iota(jnp.int32, (RT, RT), 0)
    j = lax.broadcasted_iota(jnp.int32, (RT, RT), 1)
    target = (i // 64) * 64 + ((i // 4) % 2) * 32 + ((i // 8) % 8) * 4 + i % 4
    return (target == j).astype(BF16)


def per_device(measured, view_mask, tex_factor, view_factor, light_factor, core_tensor):
    tex_count = lax.axis_size(TEX)
    tex_rows, views = measured.shape[:2]
    core_rows, band = core_tensor.shape[:2]
    width = band * RL
    texels_all = tex_rows * tex_count
    scaling = (RT * RV * RL) ** (-0.5)
    rate_tex = RT / (VALID * L)
    rate_view = RV / (texels_all * L)
    rate_core = RT * RV * RL / (texels_all * VALID * L)
    nx, nzl, nc, ny, nzh = SIZES
    bands = ny * nzh
    near = nzl * core_rows
    weights = view_mask.astype(F32)[:, None, None]
    order = column_order()
    tex_bf = jnp.dot(tex_factor.astype(BF16), order, preferred_element_type=F32).astype(BF16)
    view_bands = view_factor.astype(BF16).reshape(views, bands, band)
    core_bf = core_tensor.astype(BF16).reshape(core_rows, width)

    core_z = gather_blocks(core_bf, ("zh", "zl")).reshape(nzh, near, width)
    core_xc = gather_blocks(core_z, ("x", "c"))
    core_pair = jnp.transpose(core_xc, (1, 0, 2, 3)).reshape(nzh, RT, width)
    proj_pair = jnp.einsum("ta,zan->ztn", tex_bf, core_pair, preferred_element_type=F32)
    projected = gather_blocks(proj_pair.astype(BF16), ("y",))
    projected = projected.reshape(bands, tex_rows, band, RL)

    mixed = jnp.einsum(
        "vgb,gtbc->vtc", view_bands, projected, preferred_element_type=F32
    ).astype(BF16)
    approx = jnp.einsum("vtc,lc->vtl", mixed, light_factor, preferred_element_type=F32)
    target = jnp.transpose(measured, (1, 0, 2)).astype(F32)
    resid = (weights * (scaling * approx - target)).astype(BF16)
    back = jnp.einsum("vtl,lc->vtc", resid, light_factor, preferred_element_type=F32).astype(BF16)

    partial_y = jnp.einsum("vgb,vtc->gtbc", view_bands, back, preferred_element_type=F32)
    partial_y = partial_y.astype(BF16).reshape(ny, 1, nzh, tex_rows, width)
    partial_y = jnp.broadcast_to(partial_y, (ny, nzh, nzh, tex_rows, width))
    partial_y = partial_y.reshape(bands, nzh, tex_rows, width)
    summed = sum_blocks(exchange(partial_y, VIEW)).astype(BF16)
    view_part = jnp.einsum("vtc,gtbc->vgb", back, projected, preferred_element_type=F32)

    tex_part = jnp.einsum("ztn,zan->ta", summed, core_pair, preferred_element_type=F32)
    tex_part = lax.dot_general(
        tex_part.astype(BF16), order, (((1,), (1,)), ((), ())), preferred_element_type=F32
    )
    tex_blocks = gather_blocks(tex_part.astype(BF16), ("y",))
    grad_tex = scaling * sum_blocks(tex_blocks)

    own = jnp.where(lax.axis_index("zh") == 0, summed[0], summed[1])
    core_part = jnp.einsum("ta,tn->an", tex_bf, own, preferred_element_type=F32)
    core_part = core_part.astype(BF16).reshape(nx * nc, near, width)
    spare = core_rows * width - views * RV
    view_part = jnp.pad(view_part.astype(BF16).reshape(views * RV), (0, spare))
    view_part = view_part.reshape(core_rows, width)
    view_block = jnp.broadcast_to(view_part[None], (nx * nc, core_rows, width))
    both = exchange(jnp.concatenate([core_part, view_block], axis=1), ("x", "c"))
    both = sum_blocks(both).astype(BF16)
    core_part = both[:near].reshape(nzl, core_rows, width)
    view_block = jnp.broadcast_to(both[None, near:], (nzl, core_rows, width))
    both = exchange(jnp.concatenate([core_part, view_block], axis=1), ("zl",))
    both = scaling * sum_blocks(both)
    grad_core = both[:core_rows].reshape(core_tensor.shape)
    grad_view = both[core_rows:].reshape(core_rows * width)[: views * RV]

    return (
        tex_factor - rate_tex * grad_tex,
        view_factor - rate_view * grad_view.reshape(view_factor.shape),
        core_tensor - rate_core * grad_core,
    )


def solution(mesh):
    parts = Mesh(mesh.devices.reshape(SIZES), NAMES)
    return jax.shard_map(
        per_device,
        mesh=parts,
        in_specs=(
            P(TEX, VIEW, None),
            P(VIEW),
            P(TEX, None),
            P(VIEW, None),
            P(),
            P(TEX, VIEW, None),
        ),
        out_specs=(P(TEX, None), P(VIEW, None), P(TEX, VIEW, None)),
        check_vma=False,
    )
```

```python
import jax
import jax.numpy as jnp
from jax import lax
from jax.sharding import Mesh, PartitionSpec as P

RT = 256
RV = 64
RL = 64
VALID = 151
L = 151

F32 = jnp.float32
BF16 = jnp.bfloat16

SIZES = (4, 8, 2, 4, 2)
NAMES = ("x", "zl", "c", "y", "zh")
TEX = ("x", "zl", "c")
VIEW = ("y", "zh")


def exchange(x, axes):
    return lax.all_to_all(x, axes, 0, 0, tiled=True)


def gather_blocks(x, axes):
    count = lax.axis_size(axes)
    return exchange(jnp.broadcast_to(x[None], (count,) + x.shape), axes)


def sum_blocks(x):
    return jnp.sum(x.astype(F32), axis=0)


def column_order(flip):
    i = lax.broadcasted_iota(jnp.int32, (RT, RT), 0)
    j = lax.broadcasted_iota(jnp.int32, (RT, RT), 1)
    x, zl, c, r = i // 64, (i // 8) % 8, (i // 4) % 2, i % 4
    low = zl * 4 + r
    if flip is None:
        target = x * 64 + c * 32 + low
    else:
        target = (c ^ flip) * 128 + x * 32 + low
    return (target == j).astype(BF16)


def per_device(measured, view_mask, tex_factor, view_factor, light_factor, core_tensor):
    tex_count = lax.axis_size(TEX)
    tex_rows, views = measured.shape[:2]
    core_rows, band = core_tensor.shape[:2]
    width = band * RL
    texels_all = tex_rows * tex_count
    scaling = (RT * RV * RL) ** (-0.5)
    rate_tex = RT / (VALID * L)
    rate_view = RV / (texels_all * L)
    rate_core = RT * RV * RL / (texels_all * VALID * L)
    nx, nzl, nc, ny, nzh = SIZES
    bands = ny * nzh
    near = nzl * core_rows
    weights = view_mask.astype(F32)[:, None, None]
    view_bf = view_factor.astype(BF16)
    view_bands = view_bf.reshape(views, bands, band)
    core_bf = core_tensor.astype(BF16).reshape(core_rows, width)

    core_z = gather_blocks(core_bf, ("zh", "zl")).reshape(nzh, near, width)
    core_own = gather_blocks(core_z, ("x", "y")).reshape(nx, ny, nzh, near, width)
    core_other = lax.ppermute(core_own, "c", [(0, 1), (1, 0)])

    tex_raw = tex_factor.astype(BF16)
    order = lax.optimization_barrier(column_order(lax.axis_index("c")))
    tex_rel = jnp.dot(tex_raw, order, preferred_element_type=F32).astype(BF16)
    tex_rel = tex_rel.reshape(tex_rows, nc, nx, near)
    tex_abs = jnp.dot(tex_raw, column_order(None), preferred_element_type=F32).astype(BF16)
    tex_rel, tex_abs = lax.optimization_barrier((tex_rel, tex_abs))

    projected = jnp.einsum(
        "txk,xyzkn->yztn", tex_rel[:, 0], core_own, preferred_element_type=F32
    ) + jnp.einsum("txk,xyzkn->yztn", tex_rel[:, 1], core_other, preferred_element_type=F32)
    projected = projected.astype(BF16).reshape(bands, tex_rows, band, RL)

    mixed = jnp.einsum(
        "vgb,gtbc->vtc", view_bands, projected, preferred_element_type=F32
    ).astype(BF16)
    approx = jnp.einsum("vtc,lc->vtl", mixed, light_factor, preferred_element_type=F32)
    target = jnp.transpose(measured, (1, 0, 2)).astype(F32)
    resid = (weights * (scaling * approx - target)).astype(BF16)
    back = jnp.einsum("vtl,lc->vtc", resid, light_factor, preferred_element_type=F32).astype(BF16)

    partial_y = jnp.einsum("vgb,vtc->gtbc", view_bands, back, preferred_element_type=F32)
    partial_y = partial_y.astype(BF16).reshape(ny, nzh, tex_rows, width)
    tex_part = jnp.concatenate(
        [
            jnp.einsum("yztn,xyzkn->txk", partial_y, half, preferred_element_type=F32)
            .astype(BF16)
            .reshape(tex_rows, nx * near)
            for half in (core_own, core_other)
        ],
        axis=1,
    )
    tex_part = lax.dot_general(
        tex_part, order, (((1,), (1,)), ((), ())), preferred_element_type=F32
    ).astype(BF16)
    tex_block = jnp.broadcast_to(tex_part[None], (bands, tex_rows, RT))
    blocks = jnp.concatenate([partial_y.reshape(bands, tex_rows, width), tex_block], axis=2)
    blocks = sum_blocks(exchange(blocks, VIEW))
    summed = blocks[:, :width].astype(BF16)
    grad_tex = scaling * blocks[:, width:]
    view_part = jnp.einsum("vtc,gtbc->vgb", back, projected, preferred_element_type=F32)

    core_part = jnp.einsum("ta,tn->an", tex_abs, summed, preferred_element_type=F32)
    core_part = core_part.astype(BF16).reshape(nx * nc, near, width)
    spare = core_rows * width - views * RV
    view_part = jnp.pad(view_part.astype(BF16).reshape(views * RV), (0, spare))
    view_part = view_part.reshape(core_rows, width)
    view_block = jnp.broadcast_to(view_part[None], (nx * nc, core_rows, width))
    both = exchange(jnp.concatenate([core_part, view_block], axis=1), ("x", "c"))
    both = sum_blocks(both).astype(BF16)
    core_part = both[:near].reshape(nzl, core_rows, width)
    view_block = jnp.broadcast_to(both[None, near:], (nzl, core_rows, width))
    both = exchange(jnp.concatenate([core_part, view_block], axis=1), ("zl",))
    both = scaling * sum_blocks(both)
    grad_core = both[:core_rows].reshape(core_tensor.shape)
    grad_view = both[core_rows:].reshape(core_rows * width)[: views * RV]

    return (
        tex_factor - rate_tex * grad_tex,
        view_factor - rate_view * grad_view.reshape(view_factor.shape),
        core_tensor - rate_core * grad_core,
    )


def solution(mesh):
    parts = Mesh(mesh.devices.reshape(SIZES), NAMES)
    return jax.shard_map(
        per_device,
        mesh=parts,
        in_specs=(
            P(TEX, VIEW, None),
            P(VIEW),
            P(TEX, None),
            P(VIEW, None),
            P(),
            P(TEX, VIEW, None),
        ),
        out_specs=(P(TEX, None), P(VIEW, None), P(TEX, VIEW, None)),
        check_vma=False,
    )
```

```python
import jax
import jax.numpy as jnp
from jax import lax
from jax.sharding import Mesh, PartitionSpec as P

RT = 256
RV = 64
RL = 64
VALID = 151
L = 151

F32 = jnp.float32
BF16 = jnp.bfloat16

SIZES = (4, 8, 2, 4, 2)
NAMES = ("x", "zl", "c", "y", "zh")
TEX = ("x", "zl", "c")
VIEW = ("y", "zh")


def exchange(x, axes):
    return lax.all_to_all(x, axes, 0, 0, tiled=True)


def gather_blocks(x, axes):
    count = lax.axis_size(axes)
    return exchange(jnp.broadcast_to(x[None], (count,) + x.shape), axes)


def sum_blocks(x):
    return jnp.sum(x.astype(F32), axis=0)


def column_order(flip):
    i = lax.broadcasted_iota(jnp.int32, (RT, RT), 0)
    j = lax.broadcasted_iota(jnp.int32, (RT, RT), 1)
    x, zl, c, r = i // 64, (i // 8) % 8, (i // 4) % 2, i % 4
    low = zl * 4 + r
    if flip is None:
        target = x * 64 + c * 32 + low
    else:
        target = (c ^ flip) * 128 + x * 32 + low
    return (target == j).astype(BF16)


def per_device(measured, view_mask, tex_factor, view_factor, light_factor, core_tensor):
    tex_count = lax.axis_size(TEX)
    tex_rows, views = measured.shape[:2]
    core_rows, band = core_tensor.shape[:2]
    width = band * RL
    texels_all = tex_rows * tex_count
    scaling = (RT * RV * RL) ** (-0.5)
    rate_tex = RT / (VALID * L)
    rate_view = RV / (texels_all * L)
    rate_core = RT * RV * RL / (texels_all * VALID * L)
    nx, nzl, nc, ny, nzh = SIZES
    bands = ny * nzh
    near = nzl * core_rows
    zh = lax.axis_index("zh")
    weights = view_mask.astype(F32)

    seen = jnp.einsum(
        "vtl,lc->vtc", jnp.transpose(measured, (1, 0, 2)), light_factor, preferred_element_type=F32
    )
    seen = (weights[:, None, None] * seen).astype(BF16)
    masked_bf = (weights[:, None] * view_factor).astype(BF16)
    sent = jnp.concatenate([seen, masked_bf[:, None, :]], axis=1)
    sent = jnp.concatenate([sent[: views // 2], sent[views // 2 :]], axis=2)
    came = lax.ppermute(sent, "zh", [(0, 1), (1, 0)])
    both_halves = jnp.where(
        zh == 0, jnp.stack([sent, came]), jnp.stack([came, sent])
    )
    both_halves = jnp.concatenate([both_halves[..., :RL], both_halves[..., RL:]], axis=1)
    both_halves = both_halves.reshape(nzh * views, tex_rows + 1, RL)
    seen_all = both_halves[:, :tex_rows].astype(F32)
    masked_all = both_halves[:, tex_rows].reshape(nzh * views, bands, band)

    gram = scaling * lax.dot_general(
        light_factor, light_factor, (((0,), (0,)), ((), ())), preferred_element_type=F32
    )
    gram_high = lax.reduce_precision(gram, 8, 7)
    gram_low = (gram - gram_high).astype(BF16)
    gram_high = gram_high.astype(BF16)

    core_bf = core_tensor.astype(BF16).reshape(core_rows, width)

    core_z = gather_blocks(core_bf, ("zh", "zl")).reshape(nzh, near, width)
    core_own = gather_blocks(core_z, ("x", "y")).reshape(nx, ny, nzh, near, width)
    core_other = lax.ppermute(core_own, "c", [(0, 1), (1, 0)])

    tex_raw = tex_factor.astype(BF16)
    order = lax.optimization_barrier(column_order(lax.axis_index("c")))
    tex_rel = jnp.dot(tex_raw, order, preferred_element_type=F32).astype(BF16)
    tex_rel = tex_rel.reshape(tex_rows, nc, nx, near)
    tex_abs = jnp.dot(tex_raw, column_order(None), preferred_element_type=F32).astype(BF16)
    tex_rel, tex_abs = lax.optimization_barrier((tex_rel, tex_abs))

    projected = jnp.einsum(
        "txk,xyzkn->yztn", tex_rel[:, 0], core_own, preferred_element_type=F32
    ) + jnp.einsum("txk,xyzkn->yztn", tex_rel[:, 1], core_other, preferred_element_type=F32)
    projected = projected.astype(BF16).reshape(bands, tex_rows, band, RL)

    mixed = jnp.einsum(
        "vgb,gtbc->vtc", masked_all, projected, preferred_element_type=F32
    ).astype(BF16)
    fitted = jnp.einsum("vtc,cd->vtd", mixed, gram_high, preferred_element_type=F32)
    fitted += jnp.einsum("vtc,cd->vtd", mixed, gram_low, preferred_element_type=F32)
    back = (fitted - seen_all).astype(BF16)

    partial_y = jnp.einsum("vgb,vtc->gtbc", masked_all, back, preferred_element_type=F32)
    partial_y = partial_y.astype(BF16).reshape(ny, nzh, tex_rows, width)
    tex_part = jnp.concatenate(
        [
            jnp.einsum("yztn,xyzkn->txk", partial_y, half, preferred_element_type=F32)
            .astype(BF16)
            .reshape(tex_rows, nx * near)
            for half in (core_own, core_other)
        ],
        axis=1,
    )
    tex_part = lax.dot_general(
        tex_part, order, (((1,), (1,)), ((), ())), preferred_element_type=F32
    ).astype(BF16)
    tex_block = jnp.broadcast_to(tex_part[None], (ny, tex_rows, RT))
    own_y = jnp.where(zh == 0, partial_y[:, 0], partial_y[:, 1])
    blocks = jnp.concatenate([own_y, tex_block], axis=2)
    blocks = sum_blocks(exchange(blocks, ("y",)))
    summed = blocks[:, :width].astype(BF16)
    grad_tex = scaling * blocks[:, width:]
    own_back = jnp.where(zh == 0, back[:views], back[views:])
    view_part = jnp.einsum("vtc,gtbc->vgb", own_back, projected, preferred_element_type=F32)

    core_part = jnp.einsum("ta,tn->an", tex_abs, summed, preferred_element_type=F32)
    core_part = core_part.astype(BF16).reshape(nx * nc, near, width)
    spare = core_rows * width - views * RV
    view_part = jnp.pad(view_part.astype(BF16).reshape(views * RV), (0, spare))
    view_part = view_part.reshape(core_rows, width)
    view_block = jnp.broadcast_to(view_part[None], (nx * nc, core_rows, width))
    both = exchange(jnp.concatenate([core_part, view_block], axis=1), ("x", "c"))
    both = sum_blocks(both).astype(BF16)
    core_part = both[:near].reshape(nzl, core_rows, width)
    view_block = jnp.broadcast_to(both[None, near:], (nzl, core_rows, width))
    both = exchange(jnp.concatenate([core_part, view_block], axis=1), ("zl",))
    both = scaling * sum_blocks(both)
    grad_core = both[:core_rows].reshape(core_tensor.shape)
    grad_view = both[core_rows:].reshape(core_rows * width)[: views * RV]

    return (
        tex_factor - rate_tex * grad_tex,
        view_factor - rate_view * grad_view.reshape(view_factor.shape),
        core_tensor - rate_core * grad_core,
    )


def solution(mesh):
    parts = Mesh(mesh.devices.reshape(SIZES), NAMES)
    return jax.shard_map(
        per_device,
        mesh=parts,
        in_specs=(
            P(TEX, VIEW, None),
            P(VIEW),
            P(TEX, None),
            P(VIEW, None),
            P(),
            P(TEX, VIEW, None),
        ),
        out_specs=(P(TEX, None), P(VIEW, None), P(TEX, VIEW, None)),
        check_vma=False,
    )
```

```python
import jax
import jax.numpy as jnp
from jax import lax
from jax.experimental import pallas as pl
from jax.experimental.pallas import tpu as pltpu
from jax.sharding import Mesh, PartitionSpec as P

RT = 256
RV = 64
RL = 64
VALID = 151
L = 151

F32 = jnp.float32
BF16 = jnp.bfloat16

SIZES = (4, 8, 2, 4, 2)
NAMES = ("x", "zl", "c", "y", "zh")
TEX = ("x", "zl", "c")
VIEW = ("y", "zh")


def exchange(x, axes):
    return lax.all_to_all(x, axes, 0, 0, tiled=True)


def gather_blocks(x, axes):
    count = lax.axis_size(axes)
    return exchange(jnp.broadcast_to(x[None], (count,) + x.shape), axes)


def sum_blocks(x):
    return jnp.sum(x.astype(F32), axis=0)


def column_order(flip):
    i = lax.broadcasted_iota(jnp.int32, (RT, RT), 0)
    j = lax.broadcasted_iota(jnp.int32, (RT, RT), 1)
    x, zl, c, r = i // 64, (i // 8) % 8, (i // 4) % 2, i % 4
    low = zl * 4 + r
    if flip is None:
        target = x * 64 + c * 32 + low
    else:
        target = (c ^ flip) * 128 + x * 32 + low
    return (target == j).astype(BF16)


def dot(a, b):
    return jnp.dot(a, b, preferred_element_type=F32)


def dot_t(a, b):
    return lax.dot_general(a, b, (((1,), (1,)), ((), ())), preferred_element_type=F32)


def same(shape, left, right):
    return lax.broadcasted_iota(jnp.int32, shape, 0) // left == (
        lax.broadcasted_iota(jnp.int32, shape, 1) // right
    )


def middle_kernel(
    zh_ref, own_ref, other_ref, tex_ref, order_ref, seen_ref, factor_ref, high_ref, low_ref,
    blocks_ref, view_ref,
):
    sub = 8
    nx, ny, nzh = SIZES[0], SIZES[3], SIZES[4]
    pairs, both, width = own_ref.shape
    near = both // nzh
    rows = tex_ref.shape[0]
    band = width // RL
    groups = rows // sub
    views = factor_ref.shape[0]
    factor = factor_ref[...].astype(F32)

    spread_v = jnp.where(same((views * sub, views), sub, 1), 1.0, 0.0).astype(BF16)
    spread_b = jnp.where(same((RV * sub, RV), sub, 1), 1.0, 0.0).astype(BF16)
    tall = dot_t(dot(spread_v, factor.astype(BF16)).astype(BF16), spread_b)
    r = lax.broadcasted_iota(jnp.int32, tall.shape, 0) % sub
    c = lax.broadcasted_iota(jnp.int32, tall.shape, 1) % sub
    eye = r == c
    tall = jnp.where(eye, tall, 0.0).astype(BF16)
    wide = dot_t(dot_t(spread_b, factor.astype(BF16)).astype(BF16), spread_v)
    r = lax.broadcasted_iota(jnp.int32, wide.shape, 0) % sub
    c = lax.broadcasted_iota(jnp.int32, wide.shape, 1) % sub
    wide = jnp.where(r == c, wide, 0.0).astype(BF16)

    def core_of(g):
        y, z = g // nzh, g % nzh
        return jnp.concatenate(
            [
                ref[x * ny + y, z * near : (z + 1) * near, :]
                for ref in (own_ref, other_ref)
                for x in range(nx)
            ],
            axis=0,
        )

    tex = tex_ref[...]
    projected = [dot(tex, core_of(g)) for g in range(ny * nzh)]
    backs, ys, stacks = [], [], []
    for k in range(groups):
        stack = jnp.concatenate(
            [
                p[k * sub : (k + 1) * sub, b * RL : (b + 1) * RL]
                for p in projected
                for b in range(band)
            ],
            axis=0,
        ).astype(BF16)
        mixed = dot(tall, stack).astype(BF16)
        fitted = dot(mixed, high_ref[...]) + dot(mixed, low_ref[...])
        seen = seen_ref[:, k * sub : (k + 1) * sub, :].reshape(views * sub, RL)
        back = (fitted - seen).astype(BF16)
        stacks.append(stack)
        backs.append(back)
        ys.append(dot(wide, back))

    tex_part = None
    for g in range(ny * nzh):
        y_g = jnp.concatenate(
            [
                jnp.concatenate(
                    [y[(g * band + b) * sub : (g * band + b + 1) * sub, :] for b in range(band)],
                    axis=1,
                )
                for y in ys
            ],
            axis=0,
        ).astype(BF16)
        part = dot_t(y_g, core_of(g))
        tex_part = part if tex_part is None else tex_part + part

        @pl.when(zh_ref[0] == g % nzh)
        def _():
            blocks_ref[g // nzh, :, :width] = y_g

    tex_part = dot_t(tex_part.astype(BF16), order_ref[...]).astype(BF16)
    for y in range(ny):
        blocks_ref[y, :, width:] = tex_part

    cross = None
    for back, stack in zip(backs, stacks):
        part = dot_t(back, stack)
        cross = part if cross is None else cross + part
    cross = jnp.where(eye, cross, 0.0).astype(BF16)
    cross = lax.dot_general(
        spread_v, cross, (((0,), (0,)), ((), ())), preferred_element_type=F32
    )
    view_ref[...] = dot(cross.astype(BF16), spread_b)


def middle(zh, core_own, core_other, tex_rel, order, seen, factor, high, low):
    rows, views = tex_rel.shape[0], factor.shape[0]
    ny, width = SIZES[3], core_own.shape[-1]
    vmem = pl.BlockSpec(memory_space=pltpu.VMEM)
    return pl.pallas_call(
        middle_kernel,
        out_shape=(
            jax.ShapeDtypeStruct((ny, rows, width + RT), BF16),
            jax.ShapeDtypeStruct((views, RV), F32),
        ),
        in_specs=[pl.BlockSpec(memory_space=pltpu.SMEM)] + [vmem] * 8,
        out_specs=(vmem, vmem),
        compiler_params=pltpu.CompilerParams(vmem_limit_bytes=24 << 20),
        cost_estimate=pl.CostEstimate(flops=10**9, bytes_accessed=3 * 10**6, transcendentals=0),
        name="middle",
    )(zh.reshape(1), core_own, core_other, tex_rel, order, seen, factor, high, low)


def per_device(measured, view_mask, tex_factor, view_factor, light_factor, core_tensor):
    tex_count = lax.axis_size(TEX)
    tex_rows, views = measured.shape[:2]
    core_rows, band = core_tensor.shape[:2]
    width = band * RL
    texels_all = tex_rows * tex_count
    scaling = (RT * RV * RL) ** (-0.5)
    rate_tex = RT / (VALID * L)
    rate_view = RV / (texels_all * L)
    rate_core = RT * RV * RL / (texels_all * VALID * L)
    nx, nzl, nc, ny, nzh = SIZES
    bands = ny * nzh
    near = nzl * core_rows
    zh = lax.axis_index("zh")
    weights = view_mask.astype(F32)

    seen = jnp.einsum(
        "vtl,lc->vtc", jnp.transpose(measured, (1, 0, 2)), light_factor, preferred_element_type=F32
    )
    seen = (weights[:, None, None] * seen).astype(BF16)
    masked_bf = (weights[:, None] * view_factor).astype(BF16)
    sent = jnp.concatenate([seen, masked_bf[:, None, :]], axis=1)
    sent = jnp.concatenate([sent[: views // 2], sent[views // 2 :]], axis=2)
    came = lax.ppermute(sent, "zh", [(0, 1), (1, 0)])
    both_halves = jnp.where(
        zh == 0, jnp.stack([sent, came]), jnp.stack([came, sent])
    )
    both_halves = jnp.concatenate([both_halves[..., :RL], both_halves[..., RL:]], axis=1)
    both_halves = both_halves.reshape(nzh * views, tex_rows + 1, RL)
    seen_all = both_halves[:, :tex_rows].astype(F32)
    masked_all = both_halves[:, tex_rows]

    gram = scaling * lax.dot_general(
        light_factor, light_factor, (((0,), (0,)), ((), ())), preferred_element_type=F32
    )
    gram_high = lax.reduce_precision(gram, 8, 7)
    gram_low = (gram - gram_high).astype(BF16)
    gram_high = gram_high.astype(BF16)

    core_bf = core_tensor.astype(BF16).reshape(core_rows, width)

    core_z = gather_blocks(core_bf, ("zh", "zl")).reshape(nzh, near, width)
    core_own = gather_blocks(core_z, ("x", "y")).reshape(nx * ny, nzh * near, width)
    core_other = lax.ppermute(core_own, "c", [(0, 1), (1, 0)])

    tex_raw = tex_factor.astype(BF16)
    order = lax.optimization_barrier(column_order(lax.axis_index("c")))
    tex_rel = jnp.dot(tex_raw, order, preferred_element_type=F32).astype(BF16)
    tex_abs = jnp.dot(tex_raw, column_order(None), preferred_element_type=F32).astype(BF16)
    tex_rel, tex_abs = lax.optimization_barrier((tex_rel, tex_abs))

    blocks, view_part = middle(
        zh, core_own, core_other, tex_rel, order, seen_all, masked_all, gram_high, gram_low
    )
    blocks = sum_blocks(exchange(blocks, ("y",)))
    summed = blocks[:, :width].astype(BF16)
    grad_tex = scaling * blocks[:, width:]
    view_part = jnp.where(zh == 0, view_part[:views], view_part[views:])

    core_part = jnp.einsum("ta,tn->an", tex_abs, summed, preferred_element_type=F32)
    core_part = core_part.astype(BF16).reshape(nx * nc, near, width)
    spare = core_rows * width - views * RV
    view_part = jnp.pad(view_part.astype(BF16).reshape(views * RV), (0, spare))
    view_part = view_part.reshape(core_rows, width)
    view_block = jnp.broadcast_to(view_part[None], (nx * nc, core_rows, width))
    both = exchange(jnp.concatenate([core_part, view_block], axis=1), ("x", "c"))
    core_part = sum_blocks(both[:, :near]).astype(BF16).reshape(nzl, core_rows, width)
    view_block = sum_blocks(both[:, near:]).astype(BF16)
    view_block = jnp.broadcast_to(view_block[None], (nzl, core_rows, width))
    both = exchange(jnp.concatenate([core_part, view_block], axis=1), ("zl",))
    both = scaling * sum_blocks(both)
    grad_core = both[:core_rows].reshape(core_tensor.shape)
    grad_view = both[core_rows:].reshape(core_rows * width)[: views * RV]

    return (
        tex_factor - rate_tex * grad_tex,
        view_factor - rate_view * grad_view.reshape(view_factor.shape),
        core_tensor - rate_core * grad_core,
    )


def solution(mesh):
    parts = Mesh(mesh.devices.reshape(SIZES), NAMES)
    return jax.shard_map(
        per_device,
        mesh=parts,
        in_specs=(
            P(TEX, VIEW, None),
            P(VIEW),
            P(TEX, None),
            P(VIEW, None),
            P(),
            P(TEX, VIEW, None),
        ),
        out_specs=(P(TEX, None), P(VIEW, None), P(TEX, VIEW, None)),
        check_vma=False,
    )
```

```python
import functools

import jax
import jax.numpy as jnp
from jax import lax
from jax.experimental import pallas as pl
from jax.experimental.pallas import tpu as pltpu
from jax.sharding import Mesh, PartitionSpec as P

RT = 256
RV = 64
RL = 64
VALID = 151
L = 151

F32 = jnp.float32
BF16 = jnp.bfloat16

SIZES = (4, 8, 2, 4, 2)
NAMES = ("x", "zl", "c", "y", "zh")
TEX = ("x", "zl", "c")
VIEW = ("y", "zh")


def exchange(x, axes):
    return lax.all_to_all(x, axes, 0, 0, tiled=True)


def gather_blocks(x, axes):
    count = lax.axis_size(axes)
    return exchange(jnp.broadcast_to(x[None], (count,) + x.shape), axes)


def sum_blocks(x):
    return jnp.sum(x.astype(F32), axis=0)


def column_order(flip):
    i = lax.broadcasted_iota(jnp.int32, (RT, RT), 0)
    j = lax.broadcasted_iota(jnp.int32, (RT, RT), 1)
    x, zl, c, r = i // 64, (i // 8) % 8, (i // 4) % 2, i % 4
    return ((c ^ flip) * 128 + x * 32 + zl * 4 + r == j).astype(BF16)


def dot(a, b):
    return jnp.dot(a, b, preferred_element_type=F32)


def dot_t(a, b):
    return lax.dot_general(a, b, (((1,), (1,)), ((), ())), preferred_element_type=F32)


def same(shape, left, right):
    return lax.broadcasted_iota(jnp.int32, shape, 0) // left == (
        lax.broadcasted_iota(jnp.int32, shape, 1) // right
    )


SUB = 8
PARAMS = pltpu.CompilerParams(vmem_limit_bytes=24 << 20)
IN_VMEM = pl.BlockSpec(memory_space=pltpu.VMEM)
IN_SMEM = pl.BlockSpec(memory_space=pltpu.SMEM)


def core_band(ref, g):
    nx, ny, nzh = SIZES[0], SIZES[3], SIZES[4]
    near = ref.shape[1] // nzh
    y, z = g // nzh, g % nzh
    return [ref[x * ny + y, z * near : (z + 1) * near, :] for x in range(nx)]


def spread(n):
    return jnp.where(same((n * SUB, n), SUB, 1), 1.0, 0.0).astype(BF16)


def first_kernel(own_ref, tex_ref, factor_ref, part_ref, tall_ref, wide_ref):
    factor = factor_ref[...]
    views = factor.shape[0]
    half = tex_ref.shape[1] // 2
    tex = tex_ref[:, :half]
    for g in range(part_ref.shape[0]):
        part_ref[g] = dot(tex, jnp.concatenate(core_band(own_ref, g), axis=0))
    spread_v, spread_b = spread(views), spread(RV)
    tall = dot_t(dot(spread_v, factor).astype(BF16), spread_b)
    wide = dot_t(dot_t(spread_b, factor).astype(BF16), spread_v)
    for full, ref in ((tall, tall_ref), (wide, wide_ref)):
        r = lax.broadcasted_iota(jnp.int32, full.shape, 0) % SUB
        c = lax.broadcasted_iota(jnp.int32, full.shape, 1) % SUB
        ref[...] = jnp.where(r == c, full, 0.0).astype(BF16)


def second_kernel(
    zh_ref, own_ref, other_ref, part_ref, tall_ref, wide_ref, tex_ref, order_ref, seen_ref,
    high_ref, low_ref, blocks_ref, view_ref,
):
    ny, nzh = SIZES[3], SIZES[4]
    bands, rows, width = part_ref.shape
    band = width // RL
    views = seen_ref.shape[0]
    half = tex_ref.shape[1] // 2
    tex = tex_ref[:, half:]
    tall, wide = tall_ref[...], wide_ref[...]

    projected = [
        part_ref[g] + dot(tex, jnp.concatenate(core_band(other_ref, g), axis=0))
        for g in range(bands)
    ]
    backs, ys, stacks = [], [], []
    for k in range(rows // SUB):
        stack = jnp.concatenate(
            [
                p[k * SUB : (k + 1) * SUB, b * RL : (b + 1) * RL]
                for p in projected
                for b in range(band)
            ],
            axis=0,
        ).astype(BF16)
        mixed = dot(tall, stack).astype(BF16)
        fitted = dot(mixed, high_ref[...]) + dot(mixed, low_ref[...])
        seen = seen_ref[:, k * SUB : (k + 1) * SUB, :].reshape(views * SUB, RL)
        back = (fitted - seen).astype(BF16)
        stacks.append(stack)
        backs.append(back)
        ys.append(dot(wide, back))

    tex_part = None
    for g in range(bands):
        y_g = jnp.concatenate(
            [
                jnp.concatenate(
                    [y[(g * band + b) * SUB : (g * band + b + 1) * SUB, :] for b in range(band)],
                    axis=1,
                )
                for y in ys
            ],
            axis=0,
        ).astype(BF16)
        core = jnp.concatenate(core_band(own_ref, g) + core_band(other_ref, g), axis=0)
        part = dot_t(y_g, core)
        tex_part = part if tex_part is None else tex_part + part

        @pl.when(zh_ref[0] == g % nzh)
        def _():
            blocks_ref[g // nzh, :, :width] = y_g

    tex_part = dot_t(tex_part.astype(BF16), order_ref[...]).astype(BF16)
    for y in range(ny):
        blocks_ref[y, :, width:] = tex_part

    cross = None
    for back, stack in zip(backs, stacks):
        part = dot_t(back, stack)
        cross = part if cross is None else cross + part
    r = lax.broadcasted_iota(jnp.int32, cross.shape, 0) % SUB
    c = lax.broadcasted_iota(jnp.int32, cross.shape, 1) % SUB
    cross = jnp.where(r == c, cross, 0.0).astype(BF16)
    cross = lax.dot_general(
        spread(views), cross, (((0,), (0,)), ((), ())), preferred_element_type=F32
    )
    view_part = dot(cross.astype(BF16), spread(RV))
    height = view_ref.shape[0]
    count = views // nzh
    for z in range(nzh):

        @pl.when(zh_ref[0] == z)
        def _():
            view_ref[...] = jnp.concatenate(
                [
                    view_part[z * count + v : z * count + v + height, :]
                    for v in range(0, count, height)
                ]
                + [jnp.zeros((height, width - count // height * RL), F32)],
                axis=1,
            ).astype(BF16)


def middle(zh, core_own, core_other, tex_rel, order, seen, factor, high, low, height):
    rows, views = tex_rel.shape[0], factor.shape[0]
    ny, nzh, width = SIZES[3], SIZES[4], core_own.shape[-1]
    part, tall, wide = pl.pallas_call(
        first_kernel,
        out_shape=(
            jax.ShapeDtypeStruct((ny * nzh, rows, width), F32),
            jax.ShapeDtypeStruct((views * SUB, RV * SUB), BF16),
            jax.ShapeDtypeStruct((RV * SUB, views * SUB), BF16),
        ),
        in_specs=[IN_VMEM] * 3,
        out_specs=(IN_VMEM,) * 3,
        compiler_params=PARAMS,
        cost_estimate=pl.CostEstimate(flops=10**9, bytes_accessed=2 * 10**6, transcendentals=0),
        name="first",
    )(core_own, tex_rel, factor)
    return pl.pallas_call(
        second_kernel,
        out_shape=(
            jax.ShapeDtypeStruct((ny, rows, width + RT), BF16),
            jax.ShapeDtypeStruct((height, width), BF16),
        ),
        in_specs=[IN_SMEM] + [IN_VMEM] * 10,
        out_specs=(IN_VMEM, IN_VMEM),
        compiler_params=PARAMS,
        cost_estimate=pl.CostEstimate(flops=10**9, bytes_accessed=3 * 10**6, transcendentals=0),
        name="second",
    )(zh.reshape(1), core_own, core_other, part, tall, wide, tex_rel, order, seen, high, low)


def last_kernel(
    rates, sums_ref, blocks_ref, tex_ref, view_ref, core_ref, tex_out, view_out, core_out
):
    rate_tex, rate_view, rate_core = rates
    width = sums_ref.shape[-1]
    height = core_ref.shape[0]
    total = jnp.sum(sums_ref[...].astype(F32), axis=0)
    core_grad, view_grad = rate_core * total[:height], rate_view * total[height:]
    for b in range(core_ref.shape[1]):
        core_out[:, b, :] = core_ref[:, b, :] - core_grad[:, b * RL : (b + 1) * RL]
    for b in range(view_ref.shape[0] // height):
        at = slice(b * height, (b + 1) * height)
        view_out[at, :] = view_ref[at, :] - view_grad[:, b * RV : (b + 1) * RV]
    tex_out[...] = tex_ref[...] - rate_tex * blocks_ref[:, width:]


def last(rates, sums, blocks, tex, view, core):
    return pl.pallas_call(
        functools.partial(last_kernel, rates),
        out_shape=tuple(jax.ShapeDtypeStruct(a.shape, F32) for a in (tex, view, core)),
        in_specs=[IN_VMEM] * 5,
        out_specs=(IN_VMEM,) * 3,
        compiler_params=PARAMS,
        cost_estimate=pl.CostEstimate(flops=10**5, bytes_accessed=10**5, transcendentals=0),
        name="last",
    )(sums, blocks, tex, view, core)


def per_device(measured, view_mask, tex_factor, view_factor, light_factor, core_tensor):
    tex_count = lax.axis_size(TEX)
    tex_rows, views = measured.shape[:2]
    core_rows, band = core_tensor.shape[:2]
    width = band * RL
    texels_all = tex_rows * tex_count
    scaling = (RT * RV * RL) ** (-0.5)
    rate_tex = RT / (VALID * L)
    rate_view = RV / (texels_all * L)
    rate_core = RT * RV * RL / (texels_all * VALID * L)
    nx, nzl, nc, ny, nzh = SIZES
    bands = ny * nzh
    near = nzl * core_rows
    zh = lax.axis_index("zh")
    weights = view_mask.astype(F32)

    seen = jnp.einsum(
        "vtl,lc->vtc", jnp.transpose(measured, (1, 0, 2)), light_factor, preferred_element_type=F32
    )
    seen = (weights[:, None, None] * seen).astype(BF16)
    masked_bf = (weights[:, None] * view_factor).astype(BF16)
    sent = jnp.concatenate([seen, masked_bf[:, None, :]], axis=1)
    sent = jnp.concatenate([sent[: views // 2], sent[views // 2 :]], axis=2)
    came = lax.ppermute(sent, "zh", [(0, 1), (1, 0)])
    both_halves = jnp.where(
        zh == 0, jnp.stack([sent, came]), jnp.stack([came, sent])
    )
    both_halves = jnp.concatenate([both_halves[..., :RL], both_halves[..., RL:]], axis=1)
    both_halves = both_halves.reshape(nzh * views, tex_rows + 1, RL)
    seen_all = both_halves[:, :tex_rows].astype(F32)
    masked_all = both_halves[:, tex_rows]

    gram = scaling * lax.dot_general(
        light_factor, light_factor, (((0,), (0,)), ((), ())), preferred_element_type=F32
    )
    gram_high = lax.reduce_precision(gram, 8, 7)
    gram_low = (gram - gram_high).astype(BF16)
    gram_high = gram_high.astype(BF16)

    core_bf = core_tensor.astype(BF16).reshape(core_rows, width)

    core_z = gather_blocks(core_bf, ("zh", "zl")).reshape(nzh, near, width)
    core_own = gather_blocks(core_z, ("x", "y")).reshape(nx * ny, nzh * near, width)
    core_other = lax.ppermute(core_own, "c", [(0, 1), (1, 0)])

    tex_raw = tex_factor.astype(BF16)
    order = lax.optimization_barrier(column_order(lax.axis_index("c")))
    tex_rel = lax.optimization_barrier(dot(tex_raw, order).astype(BF16))

    blocks, view_part = middle(
        zh, core_own, core_other, tex_rel, order, seen_all, masked_all, gram_high, gram_low,
        core_rows,
    )
    blocks = sum_blocks(exchange(blocks, ("y",)))
    summed = blocks[:, :width].astype(BF16)

    half = RT // nc
    tex_abs = jnp.where(
        lax.axis_index("c") == 0,
        tex_rel,
        jnp.concatenate([tex_rel[:, half:], tex_rel[:, :half]], axis=1),
    )
    core_part = jnp.einsum("ta,tn->an", tex_abs, summed, preferred_element_type=F32)
    core_part = core_part.astype(BF16).reshape(nx * nc, near, width)
    view_block = jnp.broadcast_to(view_part[None], (nx * nc, core_rows, width))
    both = exchange(jnp.concatenate([core_part, view_block], axis=1), ("c", "x"))
    core_part = sum_blocks(both[:, :near]).astype(BF16).reshape(nzl, core_rows, width)
    view_block = sum_blocks(both[:, near:]).astype(BF16)
    view_block = jnp.broadcast_to(view_block[None], (nzl, core_rows, width))
    both = exchange(jnp.concatenate([core_part, view_block], axis=1), ("zl",))
    rates = (scaling * rate_tex, scaling * rate_view, scaling * rate_core)
    return last(rates, both, blocks, tex_factor, view_factor, core_tensor)


def solution(mesh):
    parts = Mesh(mesh.devices.reshape(SIZES), NAMES)
    return jax.shard_map(
        per_device,
        mesh=parts,
        in_specs=(
            P(TEX, VIEW, None),
            P(VIEW),
            P(TEX, None),
            P(VIEW, None),
            P(),
            P(TEX, VIEW, None),
        ),
        out_specs=(P(TEX, None), P(VIEW, None), P(TEX, VIEW, None)),
        check_vma=False,
    )
```

```python
import functools

import jax
import jax.numpy as jnp
from jax import lax
from jax.experimental import pallas as pl
from jax.experimental.pallas import tpu as pltpu
from jax.sharding import Mesh, PartitionSpec as P

RT = 256
RV = 64
RL = 64
VALID = 151
L = 151

F32 = jnp.float32
BF16 = jnp.bfloat16

SIZES = (4, 8, 2, 4, 2)
NAMES = ("x", "zl", "c", "y", "zh")
TEX = ("x", "zl", "c")
VIEW = ("y", "zh")


def exchange(x, axes):
    return lax.all_to_all(x, axes, 0, 0, tiled=True)


def gather_blocks(x, axes):
    count = lax.axis_size(axes)
    return exchange(jnp.broadcast_to(x[None], (count,) + x.shape), axes)


def sum_blocks(x):
    return jnp.sum(x.astype(F32), axis=0)


def column_order(flip):
    i = lax.broadcasted_iota(jnp.int32, (RT, RT), 0)
    j = lax.broadcasted_iota(jnp.int32, (RT, RT), 1)
    x, zl, c, r = i // 64, (i // 8) % 8, (i // 4) % 2, i % 4
    return ((c ^ flip) * 128 + x * 32 + zl * 4 + r == j).astype(BF16)


def dot(a, b):
    return jnp.dot(a, b, preferred_element_type=F32)


def dot_t(a, b):
    return lax.dot_general(a, b, (((1,), (1,)), ((), ())), preferred_element_type=F32)


def same(shape, left, right):
    return lax.broadcasted_iota(jnp.int32, shape, 0) // left == (
        lax.broadcasted_iota(jnp.int32, shape, 1) // right
    )


SUB = 8
PARAMS = pltpu.CompilerParams(vmem_limit_bytes=24 << 20)
IN_VMEM = pl.BlockSpec(memory_space=pltpu.VMEM)
IN_SMEM = pl.BlockSpec(memory_space=pltpu.SMEM)


def core_band(ref, g):
    nx, ny, nzh = SIZES[0], SIZES[3], SIZES[4]
    near = ref.shape[1] // nzh
    y, z = g // nzh, g % nzh
    return [ref[x * ny + y, z * near : (z + 1) * near, :] for x in range(nx)]


def spread(n):
    return jnp.where(same((n * SUB, n), SUB, 1), 1.0, 0.0).astype(BF16)


def joined(pieces):
    return jnp.concatenate(pieces, axis=1)


def stacked(pieces):
    return jnp.concatenate(pieces, axis=0)


def diagonal(x):
    r = lax.broadcasted_iota(jnp.int32, x.shape, 0) % SUB
    c = lax.broadcasted_iota(jnp.int32, x.shape, 1) % SUB
    return jnp.where(r == c, x, 0.0).astype(BF16)


def first_kernel(
    zh_ref, own_ref, tex_ref, sent_ref, came_ref, high_ref, low_ref,
    part_ref, tall_ref, wide_ref, seen_ref, high_out, low_out,
):
    nzh = SIZES[4]
    rows = part_ref.shape[1]
    groups = rows // SUB
    half = tex_ref.shape[1] // 2
    tex = tex_ref[:, :half]
    for g in range(part_ref.shape[0]):
        part_ref[g] = dot(tex, stacked(core_band(own_ref, g)))

    count = sent_ref.shape[0] // (rows + 1)
    first_half = zh_ref[0] == 0
    sent, came = sent_ref[...].astype(F32), came_ref[...].astype(F32)
    factor, at = [], 0
    for z in range(nzh):
        side = jnp.where(first_half, sent if z == 0 else came, came if z == 0 else sent)
        for lane in range(2):
            lanes = slice(lane * RL, (lane + 1) * RL)
            for i in range(count):
                low = i * rows
                seen_ref[at : at + SUB, :] = joined(
                    [side[low + k * SUB : low + (k + 1) * SUB, lanes] for k in range(groups)]
                )
                at += SUB
            factor.append(side[count * rows :, lanes])
    factor = stacked(factor).astype(BF16)

    spread_v, spread_b = spread(factor.shape[0]), spread(RV)
    tall_ref[...] = diagonal(dot_t(dot(spread_v, factor).astype(BF16), spread_b))
    wide_ref[...] = diagonal(dot_t(dot_t(spread_b, factor).astype(BF16), spread_v))

    for ref, out in ((high_ref, high_out), (low_ref, low_out)):
        gram = ref[...]
        zero = jnp.zeros_like(gram)
        out[...] = stacked(
            [joined([gram if i == k else zero for i in range(groups)]) for k in range(groups)]
        ).astype(BF16)


def second_kernel(
    zh_ref, own_ref, other_ref, part_ref, tall_ref, wide_ref, tex_ref, order_ref, seen_ref,
    high_ref, low_ref, blocks_ref, back_ref, stack_ref,
):
    ny, nzh = SIZES[3], SIZES[4]
    bands, rows, width = part_ref.shape
    band = width // RL
    groups = rows // SUB
    half = tex_ref.shape[1] // 2
    tex = tex_ref[:, half:]

    pieces = []
    for g in range(bands):
        p = part_ref[g] + dot(tex, stacked(core_band(other_ref, g)))
        for b in range(band):
            pieces.append(
                joined(
                    [
                        p[k * SUB : (k + 1) * SUB, b * RL : (b + 1) * RL]
                        for k in range(groups)
                    ]
                )
            )
    stack = stacked(pieces).astype(BF16)
    mixed = dot(tall_ref[...], stack).astype(BF16)
    fitted = dot(mixed, high_ref[...]) + dot(mixed, low_ref[...])
    back = (fitted - seen_ref[...]).astype(BF16)
    y = dot(wide_ref[...], back)
    stack_ref[...] = stack
    back_ref[...] = back

    first_half = zh_ref[0] == 0
    tex_part, near = None, None
    for g in range(bands):
        y_g = stacked(
            [
                joined(
                    [
                        y[(g * band + b) * SUB : (g * band + b + 1) * SUB, k * RL : (k + 1) * RL]
                        for b in range(band)
                    ]
                )
                for k in range(groups)
            ]
        )
        if g % nzh == 0:
            near = y_g
        else:
            blocks_ref[g // nzh, :, :width] = jnp.where(first_half, near, y_g).astype(BF16)
        core = stacked(core_band(own_ref, g) + core_band(other_ref, g))
        part = dot_t(y_g.astype(BF16), core)
        tex_part = part if tex_part is None else tex_part + part

    tex_part = dot_t(tex_part.astype(BF16), order_ref[...]).astype(BF16)
    for i in range(ny):
        blocks_ref[i, :, width:] = tex_part


def third_kernel(zh_ref, back_ref, stack_ref, view_ref):
    height, width = view_ref.shape
    views = back_ref.shape[0] // SUB
    cross = diagonal(dot_t(back_ref[...], stack_ref[...]))
    cross = lax.dot_general(
        spread(views), cross, (((0,), (0,)), ((), ())), preferred_element_type=F32
    )
    view_part = dot(cross.astype(BF16), spread(RV))
    count = views // SIZES[4]
    own = jnp.where(zh_ref[0] == 0, view_part[:count], view_part[count:])
    view_ref[...] = joined(
        [own[v : v + height, :] for v in range(0, count, height)]
        + [jnp.zeros((height, width - count // height * RL), F32)]
    ).astype(BF16)


def cost(flops):
    return pl.CostEstimate(flops=flops, bytes_accessed=flops // 500, transcendentals=0)


def middle(zh, core_own, core_other, tex_rel, order, sent, came, high, low, height):
    rows = tex_rel.shape[0]
    ny, nzh, width = SIZES[3], SIZES[4], core_own.shape[-1]
    views = sent.shape[0] // (rows + 1) * 2 * nzh
    lanes = rows // SUB * RL
    zh = zh.reshape(1)
    part, tall, wide, seen, high, low = pl.pallas_call(
        first_kernel,
        out_shape=(
            jax.ShapeDtypeStruct((ny * nzh, rows, width), F32),
            jax.ShapeDtypeStruct((views * SUB, RV * SUB), BF16),
            jax.ShapeDtypeStruct((RV * SUB, views * SUB), BF16),
            jax.ShapeDtypeStruct((views * SUB, lanes), F32),
            jax.ShapeDtypeStruct((lanes, lanes), BF16),
            jax.ShapeDtypeStruct((lanes, lanes), BF16),
        ),
        in_specs=[IN_SMEM] + [IN_VMEM] * 6,
        out_specs=(IN_VMEM,) * 6,
        compiler_params=PARAMS,
        cost_estimate=cost(10**9),
        name="first",
    )(zh, core_own, tex_rel, sent, came, high, low)
    blocks, back, stack = pl.pallas_call(
        second_kernel,
        out_shape=(
            jax.ShapeDtypeStruct((ny, rows, width + RT), BF16),
            jax.ShapeDtypeStruct((views * SUB, lanes), BF16),
            jax.ShapeDtypeStruct((RV * SUB, lanes), BF16),
        ),
        in_specs=[IN_SMEM] + [IN_VMEM] * 10,
        out_specs=(IN_VMEM,) * 3,
        compiler_params=PARAMS,
        cost_estimate=cost(2 * 10**9),
        name="second",
    )(zh, core_own, core_other, part, tall, wide, tex_rel, order, seen, high, low)
    view = pl.pallas_call(
        third_kernel,
        out_shape=jax.ShapeDtypeStruct((height, width), BF16),
        in_specs=[IN_SMEM] + [IN_VMEM] * 2,
        out_specs=IN_VMEM,
        compiler_params=PARAMS,
        cost_estimate=cost(10**8),
        name="third",
    )(zh, back, stack)
    return blocks, view


def last_kernel(
    rates, sums_ref, blocks_ref, tex_ref, view_ref, core_ref, tex_out, view_out, core_out
):
    rate_tex, rate_view, rate_core = rates
    width = sums_ref.shape[-1]
    height = core_ref.shape[0]
    total = jnp.sum(sums_ref[...].astype(F32), axis=0)
    core_grad, view_grad = rate_core * total[:height], rate_view * total[height:]
    for b in range(core_ref.shape[1]):
        core_out[:, b, :] = core_ref[:, b, :] - core_grad[:, b * RL : (b + 1) * RL]
    for b in range(view_ref.shape[0] // height):
        at = slice(b * height, (b + 1) * height)
        view_out[at, :] = view_ref[at, :] - view_grad[:, b * RV : (b + 1) * RV]
    tex_out[...] = tex_ref[...] - rate_tex * blocks_ref[:, width:]


def last(rates, sums, blocks, tex, view, core):
    return pl.pallas_call(
        functools.partial(last_kernel, rates),
        out_shape=tuple(jax.ShapeDtypeStruct(a.shape, F32) for a in (tex, view, core)),
        in_specs=[IN_VMEM] * 5,
        out_specs=(IN_VMEM,) * 3,
        compiler_params=PARAMS,
        cost_estimate=pl.CostEstimate(flops=10**5, bytes_accessed=10**5, transcendentals=0),
        name="last",
    )(sums, blocks, tex, view, core)


def per_device(measured, view_mask, tex_factor, view_factor, light_factor, core_tensor):
    tex_count = lax.axis_size(TEX)
    tex_rows, views = measured.shape[:2]
    core_rows, band = core_tensor.shape[:2]
    width = band * RL
    texels_all = tex_rows * tex_count
    scaling = (RT * RV * RL) ** (-0.5)
    rate_tex = RT / (VALID * L)
    rate_view = RV / (texels_all * L)
    rate_core = RT * RV * RL / (texels_all * VALID * L)
    nx, nzl, nc, ny, nzh = SIZES
    bands = ny * nzh
    near = nzl * core_rows
    zh = lax.axis_index("zh")
    weights = view_mask.astype(F32)

    seen = jnp.einsum(
        "vtl,lc->vtc", jnp.transpose(measured, (1, 0, 2)), light_factor, preferred_element_type=F32
    )
    seen = (weights[:, None, None] * seen).astype(BF16)
    masked_bf = (weights[:, None] * view_factor).astype(BF16)
    sent = jnp.concatenate(
        [
            jnp.concatenate([seen[: views // 2], seen[views // 2 :]], axis=2).reshape(-1, 2 * RL),
            jnp.concatenate([masked_bf[: views // 2], masked_bf[views // 2 :]], axis=1),
        ]
    )
    came = lax.ppermute(sent, "zh", [(0, 1), (1, 0)])

    gram = scaling * lax.dot_general(
        light_factor, light_factor, (((0,), (0,)), ((), ())), preferred_element_type=F32
    )
    gram_high = lax.reduce_precision(gram, 8, 7)
    gram_low = gram - gram_high

    core_bf = core_tensor.astype(BF16).reshape(core_rows, width)

    core_z = gather_blocks(core_bf, ("zh", "zl")).reshape(nzh, near, width)
    core_own = gather_blocks(core_z, ("x", "y")).reshape(nx * ny, nzh * near, width)
    core_other = lax.ppermute(core_own, "c", [(0, 1), (1, 0)])

    tex_raw = tex_factor.astype(BF16)
    order = lax.optimization_barrier(column_order(lax.axis_index("c")))
    tex_rel = lax.optimization_barrier(dot(tex_raw, order).astype(BF16))

    blocks, view_part = middle(
        zh, core_own, core_other, tex_rel, order, sent, came, gram_high, gram_low, core_rows
    )
    blocks = sum_blocks(exchange(blocks, ("y",)))
    summed = blocks[:, :width].astype(BF16)

    half = RT // nc
    tex_abs = jnp.where(
        lax.axis_index("c") == 0,
        tex_rel,
        jnp.concatenate([tex_rel[:, half:], tex_rel[:, :half]], axis=1),
    )
    core_part = jnp.einsum("ta,tn->an", tex_abs, summed, preferred_element_type=F32)
    core_part = core_part.astype(BF16).reshape(nx * nc, near, width)
    view_block = jnp.broadcast_to(view_part[None], (nx * nc, core_rows, width))
    both = exchange(jnp.concatenate([core_part, view_block], axis=1), ("c", "x"))
    core_part = sum_blocks(both[:, :near]).astype(BF16).reshape(nzl, core_rows, width)
    view_block = sum_blocks(both[:, near:]).astype(BF16)
    view_block = jnp.broadcast_to(view_block[None], (nzl, core_rows, width))
    both = exchange(jnp.concatenate([core_part, view_block], axis=1), ("zl",))
    rates = (scaling * rate_tex, scaling * rate_view, scaling * rate_core)
    return last(rates, both, blocks, tex_factor, view_factor, core_tensor)


def solution(mesh):
    parts = Mesh(mesh.devices.reshape(SIZES), NAMES)
    return jax.shard_map(
        per_device,
        mesh=parts,
        in_specs=(
            P(TEX, VIEW, None),
            P(VIEW),
            P(TEX, None),
            P(VIEW, None),
            P(),
            P(TEX, VIEW, None),
        ),
        out_specs=(P(TEX, None), P(VIEW, None), P(TEX, VIEW, None)),
        check_vma=False,
    )
```

```python
import functools

import jax
import jax.numpy as jnp
from jax import lax
from jax.experimental import pallas as pl
from jax.experimental.pallas import tpu as pltpu
from jax.sharding import Mesh, PartitionSpec as P

RT = 256
RV = 64
RL = 64
VALID = 151
L = 151

F32 = jnp.float32
BF16 = jnp.bfloat16

SIZES = (4, 8, 2, 4, 2)
NAMES = ("x", "zl", "c", "y", "zh")
TEX = ("x", "zl", "c")
VIEW = ("y", "zh")


def exchange(x, axes):
    return lax.all_to_all(x, axes, 0, 0, tiled=True)


def gather_blocks(x, axes):
    count = lax.axis_size(axes)
    return exchange(jnp.broadcast_to(x[None], (count,) + x.shape), axes)


def sum_blocks(x):
    return jnp.sum(x.astype(F32), axis=0)


def column_order(flip):
    i = lax.broadcasted_iota(jnp.int32, (RT, RT), 0)
    j = lax.broadcasted_iota(jnp.int32, (RT, RT), 1)
    x, zl, c, r = i // 64, (i // 8) % 8, (i // 4) % 2, i % 4
    return ((c ^ flip) * 128 + x * 32 + zl * 4 + r == j).astype(BF16)


def dot(a, b):
    return jnp.dot(a, b, preferred_element_type=F32)


def dot_t(a, b):
    return lax.dot_general(a, b, (((1,), (1,)), ((), ())), preferred_element_type=F32)


def same(shape, left, right):
    return lax.broadcasted_iota(jnp.int32, shape, 0) // left == (
        lax.broadcasted_iota(jnp.int32, shape, 1) // right
    )


SUB = 8
PARAMS = pltpu.CompilerParams(vmem_limit_bytes=24 << 20)
IN_VMEM = pl.BlockSpec(memory_space=pltpu.VMEM)
IN_SMEM = pl.BlockSpec(memory_space=pltpu.SMEM)


def core_band(ref, g):
    nx, ny, nzh = SIZES[0], SIZES[3], SIZES[4]
    near = ref.shape[1] // nzh
    y, z = g // nzh, g % nzh
    return [ref[x * ny + y, z * near : (z + 1) * near, :] for x in range(nx)]


def spread(n):
    return jnp.where(same((n * SUB, n), SUB, 1), 1.0, 0.0).astype(BF16)


def joined(pieces):
    return jnp.concatenate(pieces, axis=1)


def stacked(pieces):
    return jnp.concatenate(pieces, axis=0)


def diagonal(x):
    r = lax.broadcasted_iota(jnp.int32, x.shape, 0) % SUB
    c = lax.broadcasted_iota(jnp.int32, x.shape, 1) % SUB
    return jnp.where(r == c, x, 0.0).astype(BF16)


def first_kernel(
    zh_ref, own_ref, tex_ref, sent_ref, came_ref, high_ref, low_ref,
    part_ref, tall_ref, wide_ref, seen_ref, high_out, low_out,
):
    nzh = SIZES[4]
    rows = part_ref.shape[1]
    groups = rows // SUB
    half = tex_ref.shape[1] // 2
    tex = tex_ref[:, :half]
    for g in range(part_ref.shape[0]):
        part_ref[g] = dot(tex, stacked(core_band(own_ref, g)))

    count = sent_ref.shape[0] // (rows + 1)
    first_half = zh_ref[0] == 0
    sent, came = sent_ref[...].astype(F32), came_ref[...].astype(F32)
    factor, at = [], 0
    for z in range(nzh):
        side = jnp.where(first_half, sent if z == 0 else came, came if z == 0 else sent)
        for lane in range(2):
            lanes = slice(lane * RL, (lane + 1) * RL)
            for i in range(count):
                low = i * rows
                seen_ref[at : at + SUB, :] = joined(
                    [side[low + k * SUB : low + (k + 1) * SUB, lanes] for k in range(groups)]
                )
                at += SUB
            factor.append(side[count * rows :, lanes])
    factor = stacked(factor).astype(BF16)

    spread_v, spread_b = spread(factor.shape[0]), spread(RV)
    tall_ref[...] = diagonal(dot_t(dot(spread_v, factor).astype(BF16), spread_b))
    wide_ref[...] = diagonal(dot_t(dot_t(spread_b, factor).astype(BF16), spread_v))

    for ref, out in ((high_ref, high_out), (low_ref, low_out)):
        gram = ref[...]
        zero = jnp.zeros_like(gram)
        out[...] = stacked(
            [joined([gram if i == k else zero for i in range(groups)]) for k in range(groups)]
        ).astype(BF16)


def second_kernel(
    zh_ref, own_ref, other_ref, part_ref, tall_ref, wide_ref, tex_ref, order_ref, seen_ref,
    high_ref, low_ref, blocks_ref, view_ref,
):
    ny, nzh = SIZES[3], SIZES[4]
    bands, rows, width = part_ref.shape
    band = width // RL
    groups = rows // SUB
    half = tex_ref.shape[1] // 2
    tex = tex_ref[:, half:]

    pieces = []
    for g in range(bands):
        p = part_ref[g] + dot(tex, stacked(core_band(other_ref, g)))
        for b in range(band):
            pieces.append(
                joined(
                    [
                        p[k * SUB : (k + 1) * SUB, b * RL : (b + 1) * RL]
                        for k in range(groups)
                    ]
                )
            )
    stack = stacked(pieces).astype(BF16)
    mixed = dot(tall_ref[...], stack).astype(BF16)
    fitted = dot(mixed, high_ref[...]) + dot(mixed, low_ref[...])
    back = (fitted - seen_ref[...]).astype(BF16)
    y = dot(wide_ref[...], back)

    first_half = zh_ref[0] == 0
    tex_part, near = None, None
    for g in range(bands):
        y_g = stacked(
            [
                joined(
                    [
                        y[(g * band + b) * SUB : (g * band + b + 1) * SUB, k * RL : (k + 1) * RL]
                        for b in range(band)
                    ]
                )
                for k in range(groups)
            ]
        )
        if g % nzh == 0:
            near = y_g
        else:
            blocks_ref[g // nzh, :, :width] = jnp.where(first_half, near, y_g).astype(BF16)
        core = stacked(core_band(own_ref, g) + core_band(other_ref, g))
        part = dot_t(y_g.astype(BF16), core)
        tex_part = part if tex_part is None else tex_part + part

    tex_part = dot_t(tex_part.astype(BF16), order_ref[...]).astype(BF16)
    for i in range(ny):
        blocks_ref[i, :, width:] = tex_part

    height = view_ref.shape[1]
    views = back.shape[0] // SUB
    cross = diagonal(dot_t(back, stack))
    cross = lax.dot_general(
        spread(views), cross, (((0,), (0,)), ((), ())), preferred_element_type=F32
    )
    view_part = dot(cross.astype(BF16), spread(RV))
    count = views // nzh
    own = jnp.where(first_half, view_part[:count], view_part[count:])
    own = joined(
        [own[v : v + height, :] for v in range(0, count, height)]
        + [jnp.zeros((height, width - count // height * RL), F32)]
    ).astype(BF16)
    for i in range(view_ref.shape[0]):
        view_ref[i] = own


def cost(flops):
    return pl.CostEstimate(flops=flops, bytes_accessed=flops // 500, transcendentals=0)


def middle(zh, core_own, core_other, tex_rel, order, sent, came, high, low, height):
    rows = tex_rel.shape[0]
    ny, nzh, width = SIZES[3], SIZES[4], core_own.shape[-1]
    views = sent.shape[0] // (rows + 1) * 2 * nzh
    lanes = rows // SUB * RL
    zh = zh.reshape(1)
    part, tall, wide, seen, high, low = pl.pallas_call(
        first_kernel,
        out_shape=(
            jax.ShapeDtypeStruct((ny * nzh, rows, width), F32),
            jax.ShapeDtypeStruct((views * SUB, RV * SUB), BF16),
            jax.ShapeDtypeStruct((RV * SUB, views * SUB), BF16),
            jax.ShapeDtypeStruct((views * SUB, lanes), F32),
            jax.ShapeDtypeStruct((lanes, lanes), BF16),
            jax.ShapeDtypeStruct((lanes, lanes), BF16),
        ),
        in_specs=[IN_SMEM] + [IN_VMEM] * 6,
        out_specs=(IN_VMEM,) * 6,
        compiler_params=PARAMS,
        cost_estimate=cost(10**9),
        name="first",
    )(zh, core_own, tex_rel, sent, came, high, low)
    return pl.pallas_call(
        second_kernel,
        out_shape=(
            jax.ShapeDtypeStruct((ny, rows, width + RT), BF16),
            jax.ShapeDtypeStruct((SIZES[0] * SIZES[2], height, width), BF16),
        ),
        in_specs=[IN_SMEM] + [IN_VMEM] * 10,
        out_specs=(IN_VMEM,) * 2,
        compiler_params=PARAMS,
        cost_estimate=cost(2 * 10**9),
        name="second",
    )(zh, core_own, core_other, part, tall, wide, tex_rel, order, seen, high, low)


def last_kernel(
    rates, sums_ref, blocks_ref, tex_ref, view_ref, core_ref, tex_out, view_out, core_out
):
    rate_tex, rate_view, rate_core = rates
    width = sums_ref.shape[-1]
    height = core_ref.shape[0]
    total = jnp.sum(sums_ref[...].astype(F32), axis=0)
    core_grad, view_grad = rate_core * total[:height], rate_view * total[height:]
    for b in range(core_ref.shape[1]):
        core_out[:, b, :] = core_ref[:, b, :] - core_grad[:, b * RL : (b + 1) * RL]
    for b in range(view_ref.shape[0] // height):
        at = slice(b * height, (b + 1) * height)
        view_out[at, :] = view_ref[at, :] - view_grad[:, b * RV : (b + 1) * RV]
    tex_out[...] = tex_ref[...] - rate_tex * blocks_ref[:, width:]


def last(rates, sums, blocks, tex, view, core):
    return pl.pallas_call(
        functools.partial(last_kernel, rates),
        out_shape=tuple(jax.ShapeDtypeStruct(a.shape, F32) for a in (tex, view, core)),
        in_specs=[IN_VMEM] * 5,
        out_specs=(IN_VMEM,) * 3,
        compiler_params=PARAMS,
        cost_estimate=pl.CostEstimate(flops=10**5, bytes_accessed=10**5, transcendentals=0),
        name="last",
    )(sums, blocks, tex, view, core)


def per_device(measured, view_mask, tex_factor, view_factor, light_factor, core_tensor):
    tex_count = lax.axis_size(TEX)
    tex_rows, views = measured.shape[:2]
    core_rows, band = core_tensor.shape[:2]
    width = band * RL
    texels_all = tex_rows * tex_count
    scaling = (RT * RV * RL) ** (-0.5)
    rate_tex = RT / (VALID * L)
    rate_view = RV / (texels_all * L)
    rate_core = RT * RV * RL / (texels_all * VALID * L)
    nx, nzl, nc, ny, nzh = SIZES
    bands = ny * nzh
    near = nzl * core_rows
    zh = lax.axis_index("zh")
    core_bf = core_tensor.astype(BF16).reshape(core_rows, width)

    core_z = gather_blocks(core_bf, ("zh", "zl")).reshape(nzh, near, width)
    weights = view_mask.astype(F32)

    seen = jnp.einsum(
        "vtl,lc->vtc", jnp.transpose(measured, (1, 0, 2)), light_factor, preferred_element_type=F32
    )
    seen = (weights[:, None, None] * seen).astype(BF16)
    masked_bf = (weights[:, None] * view_factor).astype(BF16)
    sent = jnp.concatenate(
        [
            jnp.concatenate([seen[: views // 2], seen[views // 2 :]], axis=2).reshape(-1, 2 * RL),
            jnp.concatenate([masked_bf[: views // 2], masked_bf[views // 2 :]], axis=1),
        ]
    )
    came = lax.ppermute(sent, "zh", [(0, 1), (1, 0)])

    gram = scaling * lax.dot_general(
        light_factor, light_factor, (((0,), (0,)), ((), ())), preferred_element_type=F32
    )
    gram_high = lax.reduce_precision(gram, 8, 7)
    gram_low = gram - gram_high

    core_own = gather_blocks(core_z, ("x", "y")).reshape(nx * ny, nzh * near, width)
    core_other = lax.ppermute(core_own, "c", [(0, 1), (1, 0)])

    tex_raw = tex_factor.astype(BF16)
    order = lax.optimization_barrier(column_order(lax.axis_index("c")))
    tex_rel = dot(tex_raw, order).astype(BF16)
    half = RT // nc
    tex_abs = jnp.where(
        lax.axis_index("c") == 0,
        tex_rel,
        jnp.concatenate([tex_rel[:, half:], tex_rel[:, :half]], axis=1),
    )
    tex_rel, tex_abs = lax.optimization_barrier((tex_rel, tex_abs))

    blocks, view_part = middle(
        zh, core_own, core_other, tex_rel, order, sent, came, gram_high, gram_low, core_rows
    )
    blocks = sum_blocks(exchange(blocks, ("y",)))
    summed = blocks[:, :width].astype(BF16)

    core_part = jnp.einsum("ta,tn->an", tex_abs, summed, preferred_element_type=F32)
    core_part = core_part.astype(BF16).reshape(nx * nc, nzl, core_rows, width)
    both = exchange(jnp.concatenate([core_part, view_part[:, None]], axis=1), ("c", "x"))
    both = sum_blocks(both).astype(BF16)
    core_part, view_block = both[:nzl], both[nzl]
    view_block = jnp.broadcast_to(view_block[None], (nzl, core_rows, width))
    both = exchange(jnp.concatenate([core_part, view_block], axis=1), ("zl",))
    rates = (scaling * rate_tex, scaling * rate_view, scaling * rate_core)
    return last(rates, both, blocks, tex_factor, view_factor, core_tensor)


def solution(mesh):
    parts = Mesh(mesh.devices.reshape(SIZES), NAMES)
    return jax.shard_map(
        per_device,
        mesh=parts,
        in_specs=(
            P(TEX, VIEW, None),
            P(VIEW),
            P(TEX, None),
            P(VIEW, None),
            P(),
            P(TEX, VIEW, None),
        ),
        out_specs=(P(TEX, None), P(VIEW, None), P(TEX, VIEW, None)),
        check_vma=False,
    )
```

```python
import functools

import jax
import jax.numpy as jnp
from jax import lax
from jax.experimental import pallas as pl
from jax.experimental.pallas import tpu as pltpu
from jax.sharding import Mesh, PartitionSpec as P

RT = 256
RV = 64
RL = 64
VALID = 151
L = 151

F32 = jnp.float32
BF16 = jnp.bfloat16

SIZES = (4, 8, 2, 4, 2)
NAMES = ("x", "zl", "c", "y", "zh")
TEX = ("x", "zl", "c")
VIEW = ("y", "zh")


def exchange(x, axes):
    return lax.all_to_all(x, axes, 0, 0, tiled=True)


def gather_blocks(x, axes):
    count = lax.axis_size(axes)
    return exchange(jnp.broadcast_to(x[None], (count,) + x.shape), axes)


def sum_blocks(x):
    return jnp.sum(x.astype(F32), axis=0)


def column_order(flip):
    i = lax.broadcasted_iota(jnp.int32, (RT, RT), 0)
    j = lax.broadcasted_iota(jnp.int32, (RT, RT), 1)
    x, zl, c, r = i // 64, (i // 8) % 8, (i // 4) % 2, i % 4
    return ((c ^ flip) * 128 + x * 32 + zl * 4 + r == j).astype(BF16)


def dot(a, b):
    return jnp.dot(a, b, preferred_element_type=F32)


def dot_t(a, b):
    return lax.dot_general(a, b, (((1,), (1,)), ((), ())), preferred_element_type=F32)


def same(shape, left, right):
    return lax.broadcasted_iota(jnp.int32, shape, 0) // left == (
        lax.broadcasted_iota(jnp.int32, shape, 1) // right
    )


SUB = 8
PARAMS = pltpu.CompilerParams(vmem_limit_bytes=24 << 20)
IN_VMEM = pl.BlockSpec(memory_space=pltpu.VMEM)
IN_SMEM = pl.BlockSpec(memory_space=pltpu.SMEM)


def core_band(ref, g):
    nx, ny, nzh = SIZES[0], SIZES[3], SIZES[4]
    near = ref.shape[1] // nzh
    y, z = g // nzh, g % nzh
    return [ref[x * ny + y, z * near : (z + 1) * near, :] for x in range(nx)]


def spread(n):
    return jnp.where(same((n * SUB, n), SUB, 1), 1.0, 0.0).astype(BF16)


def joined(pieces):
    return jnp.concatenate(pieces, axis=1)


def stacked(pieces):
    return jnp.concatenate(pieces, axis=0)


def diagonal(x):
    r = lax.broadcasted_iota(jnp.int32, x.shape, 0) % SUB
    c = lax.broadcasted_iota(jnp.int32, x.shape, 1) % SUB
    return jnp.where(r == c, x, 0.0).astype(BF16)


def first_kernel(
    zh_ref, own_ref, tex_ref, sent_ref, came_ref, high_ref, low_ref,
    part_ref, tall_ref, wide_ref, seen_ref, high_out, low_out,
):
    nzh = SIZES[4]
    rows = part_ref.shape[1]
    groups = rows // SUB
    half = tex_ref.shape[1] // 2
    tex = tex_ref[:, :half]
    for g in range(part_ref.shape[0]):
        part_ref[g] = dot(tex, stacked(core_band(own_ref, g)))

    count = sent_ref.shape[0] // (rows + 1)
    first_half = zh_ref[0] == 0
    sent, came = sent_ref[...].astype(F32), came_ref[...].astype(F32)
    factor, at = [], 0
    for z in range(nzh):
        side = jnp.where(first_half, sent if z == 0 else came, came if z == 0 else sent)
        for lane in range(2):
            lanes = slice(lane * RL, (lane + 1) * RL)
            for i in range(count):
                low = i * rows
                seen_ref[at : at + SUB, :] = joined(
                    [side[low + k * SUB : low + (k + 1) * SUB, lanes] for k in range(groups)]
                )
                at += SUB
            factor.append(side[count * rows :, lanes])
    factor = stacked(factor).astype(BF16)

    spread_v, spread_b = spread(factor.shape[0]), spread(RV)
    tall_ref[...] = diagonal(dot_t(dot(spread_v, factor).astype(BF16), spread_b))
    wide_ref[...] = diagonal(dot_t(dot_t(spread_b, factor).astype(BF16), spread_v))

    for ref, out in ((high_ref, high_out), (low_ref, low_out)):
        gram = ref[...]
        zero = jnp.zeros_like(gram)
        out[...] = stacked(
            [joined([gram if i == k else zero for i in range(groups)]) for k in range(groups)]
        ).astype(BF16)


def keep(x, refs):
    refs[0][...] = x[:, :128]
    rest = x[:, 128:]
    refs[1][...] = joined([rest, jnp.zeros((rest.shape[0], 128 - rest.shape[1]), rest.dtype)])


def second_kernel(
    zh_ref, own_ref, other_ref, part_ref, tall_ref, wide_ref, tex_ref, order_ref, seen_ref,
    high_ref, low_ref, blocks_ref, view_ref, *kept,
):
    ny, nzh = SIZES[3], SIZES[4]
    back_ref, stack_ref = kept[:2], kept[2:]
    bands, rows, width = part_ref.shape
    band = width // RL
    groups = rows // SUB
    half = tex_ref.shape[1] // 2
    tex = tex_ref[:, half:]

    pieces = []
    for g in range(bands):
        p = part_ref[g] + dot(tex, stacked(core_band(other_ref, g)))
        for b in range(band):
            pieces.append(
                joined(
                    [
                        p[k * SUB : (k + 1) * SUB, b * RL : (b + 1) * RL]
                        for k in range(groups)
                    ]
                )
            )
    stack = stacked(pieces)
    keep(stack, stack_ref)
    stack = stack.astype(BF16)
    mixed = dot(tall_ref[...], stack).astype(BF16)
    fitted = dot(mixed, high_ref[...]) + dot(mixed, low_ref[...])
    back = fitted - seen_ref[...]
    keep(back, back_ref)
    back = back.astype(BF16)
    y = dot(wide_ref[...], back)

    first_half = zh_ref[0] == 0
    tex_part, near = None, None
    view_part, views = None, back.shape[0] // SUB
    for g in range(bands):
        y_g = stacked(
            [
                joined(
                    [
                        y[(g * band + b) * SUB : (g * band + b + 1) * SUB, k * RL : (k + 1) * RL]
                        for b in range(band)
                    ]
                )
                for k in range(groups)
            ]
        )
        if g % nzh == 0:
            near = y_g
        else:
            blocks_ref[g // nzh, :, :width] = jnp.where(first_half, near, y_g).astype(BF16)
        core = stacked(core_band(own_ref, g) + core_band(other_ref, g))
        part = dot_t(y_g.astype(BF16), core)
        tex_part = part if tex_part is None else tex_part + part

        for t in range(g, SUB, bands):
            left, right = (
                joined([part[pl.ds(t, n, stride=SUB), :] for part in ref]).astype(BF16)
                for ref, n in ((back_ref, views), (stack_ref, RV))
            )
            part = dot_t(left, right)
            view_part = part if view_part is None else view_part + part

    tex_part = dot_t(tex_part.astype(BF16), order_ref[...]).astype(BF16)
    for i in range(ny):
        blocks_ref[i, :, width:] = tex_part

    height = view_ref.shape[1]
    count = views // nzh
    own = jnp.where(first_half, view_part[:count], view_part[count:])
    own = joined(
        [own[v : v + height, :] for v in range(0, count, height)]
        + [jnp.zeros((height, width - count // height * RL), F32)]
    ).astype(BF16)
    for i in range(view_ref.shape[0]):
        view_ref[i] = own


def cost(flops):
    return pl.CostEstimate(flops=flops, bytes_accessed=flops // 500, transcendentals=0)


def middle(zh, core_own, core_other, tex_rel, order, sent, came, high, low, height):
    rows = tex_rel.shape[0]
    ny, nzh, width = SIZES[3], SIZES[4], core_own.shape[-1]
    views = sent.shape[0] // (rows + 1) * 2 * nzh
    lanes = rows // SUB * RL
    zh = zh.reshape(1)
    part, tall, wide, seen, high, low = pl.pallas_call(
        first_kernel,
        out_shape=(
            jax.ShapeDtypeStruct((ny * nzh, rows, width), F32),
            jax.ShapeDtypeStruct((views * SUB, RV * SUB), BF16),
            jax.ShapeDtypeStruct((RV * SUB, views * SUB), BF16),
            jax.ShapeDtypeStruct((views * SUB, lanes), F32),
            jax.ShapeDtypeStruct((lanes, lanes), BF16),
            jax.ShapeDtypeStruct((lanes, lanes), BF16),
        ),
        in_specs=[IN_SMEM] + [IN_VMEM] * 6,
        out_specs=(IN_VMEM,) * 6,
        compiler_params=PARAMS,
        cost_estimate=cost(10**9),
        name="first",
    )(zh, core_own, tex_rel, sent, came, high, low)
    return pl.pallas_call(
        second_kernel,
        out_shape=(
            jax.ShapeDtypeStruct((ny, rows, width + RT), BF16),
            jax.ShapeDtypeStruct((SIZES[0] * SIZES[2], height, width), BF16),
        ),
        in_specs=[IN_SMEM] + [IN_VMEM] * 10,
        out_specs=(IN_VMEM,) * 2,
        scratch_shapes=[
            pltpu.VMEM((n * SUB, 128), F32) for n in (views, views, RV, RV)
        ],
        compiler_params=PARAMS,
        cost_estimate=cost(2 * 10**9),
        name="second",
    )(zh, core_own, core_other, part, tall, wide, tex_rel, order, seen, high, low)


def last_kernel(
    rates, sums_ref, blocks_ref, tex_ref, view_ref, core_ref, tex_out, view_out, core_out
):
    rate_tex, rate_view, rate_core = rates
    width = sums_ref.shape[-1]
    height = core_ref.shape[0]
    total = jnp.sum(sums_ref[...].astype(F32), axis=0)
    core_grad, view_grad = rate_core * total[:height], rate_view * total[height:]
    for b in range(core_ref.shape[1]):
        core_out[:, b, :] = core_ref[:, b, :] - core_grad[:, b * RL : (b + 1) * RL]
    for b in range(view_ref.shape[0] // height):
        at = slice(b * height, (b + 1) * height)
        view_out[at, :] = view_ref[at, :] - view_grad[:, b * RV : (b + 1) * RV]
    tex_out[...] = tex_ref[...] - rate_tex * blocks_ref[:, width:]


def last(rates, sums, blocks, tex, view, core):
    return pl.pallas_call(
        functools.partial(last_kernel, rates),
        out_shape=tuple(jax.ShapeDtypeStruct(a.shape, F32) for a in (tex, view, core)),
        in_specs=[IN_VMEM] * 5,
        out_specs=(IN_VMEM,) * 3,
        compiler_params=PARAMS,
        cost_estimate=pl.CostEstimate(flops=10**5, bytes_accessed=10**5, transcendentals=0),
        name="last",
    )(sums, blocks, tex, view, core)


def per_device(measured, view_mask, tex_factor, view_factor, light_factor, core_tensor):
    tex_count = lax.axis_size(TEX)
    tex_rows, views = measured.shape[:2]
    core_rows, band = core_tensor.shape[:2]
    width = band * RL
    texels_all = tex_rows * tex_count
    scaling = (RT * RV * RL) ** (-0.5)
    rate_tex = RT / (VALID * L)
    rate_view = RV / (texels_all * L)
    rate_core = RT * RV * RL / (texels_all * VALID * L)
    nx, nzl, nc, ny, nzh = SIZES
    bands = ny * nzh
    near = nzl * core_rows
    zh = lax.axis_index("zh")
    core_bf = core_tensor.astype(BF16).reshape(core_rows, width)

    core_z = gather_blocks(core_bf, ("zh", "zl")).reshape(nzh, near, width)
    weights = view_mask.astype(F32)

    seen = jnp.einsum(
        "vtl,lc->vtc", jnp.transpose(measured, (1, 0, 2)), light_factor, preferred_element_type=F32
    )
    seen = (weights[:, None, None] * seen).astype(BF16)
    masked_bf = (weights[:, None] * view_factor).astype(BF16)
    sent = jnp.concatenate(
        [
            jnp.concatenate([seen[: views // 2], seen[views // 2 :]], axis=2).reshape(-1, 2 * RL),
            jnp.concatenate([masked_bf[: views // 2], masked_bf[views // 2 :]], axis=1),
        ]
    )
    came = lax.ppermute(sent, "zh", [(0, 1), (1, 0)])

    gram = scaling * lax.dot_general(
        light_factor, light_factor, (((0,), (0,)), ((), ())), preferred_element_type=F32
    )
    gram_high = lax.reduce_precision(gram, 8, 7)
    gram_low = gram - gram_high

    core_own = gather_blocks(core_z, ("x", "y")).reshape(nx * ny, nzh * near, width)
    core_other = lax.ppermute(core_own, "c", [(0, 1), (1, 0)])

    tex_raw = tex_factor.astype(BF16)
    order = lax.optimization_barrier(column_order(lax.axis_index("c")))
    tex_rel = dot(tex_raw, order).astype(BF16)
    half = RT // nc
    tex_abs = jnp.where(
        lax.axis_index("c") == 0,
        tex_rel,
        jnp.concatenate([tex_rel[:, half:], tex_rel[:, :half]], axis=1),
    )
    tex_rel, tex_abs = lax.optimization_barrier((tex_rel, tex_abs))

    blocks, view_part = middle(
        zh, core_own, core_other, tex_rel, order, sent, came, gram_high, gram_low, core_rows
    )
    blocks = sum_blocks(exchange(blocks, ("y",)))
    summed = blocks[:, :width].astype(BF16)

    core_part = jnp.einsum("ta,tn->an", tex_abs, summed, preferred_element_type=F32)
    core_part = core_part.astype(BF16).reshape(nx * nc, near, width)
    both = exchange(jnp.concatenate([core_part, view_part], axis=1), ("c", "x"))
    core_part = sum_blocks(both[:, :near]).astype(BF16).reshape(nzl, core_rows, width)
    view_block = sum_blocks(both[:, near:]).astype(BF16)
    view_block = jnp.broadcast_to(view_block[None], (nzl, core_rows, width))
    both = exchange(jnp.concatenate([core_part, view_block], axis=1), ("zl",))
    rates = (scaling * rate_tex, scaling * rate_view, scaling * rate_core)
    return last(rates, both, blocks, tex_factor, view_factor, core_tensor)


def solution(mesh):
    parts = Mesh(mesh.devices.reshape(SIZES), NAMES)
    return jax.shard_map(
        per_device,
        mesh=parts,
        in_specs=(
            P(TEX, VIEW, None),
            P(VIEW),
            P(TEX, None),
            P(VIEW, None),
            P(),
            P(TEX, VIEW, None),
        ),
        out_specs=(P(TEX, None), P(VIEW, None), P(TEX, VIEW, None)),
        check_vma=False,
    )
```

```python
import functools

import jax
import jax.numpy as jnp
from jax import lax
from jax.experimental import pallas as pl
from jax.experimental.pallas import tpu as pltpu
from jax.sharding import Mesh, PartitionSpec as P

RT = 256
RV = 64
RL = 64
VALID = 151
L = 151

F32 = jnp.float32
BF16 = jnp.bfloat16

SIZES = (4, 8, 2, 4, 2)
NAMES = ("x", "zl", "c", "y", "zh")
TEX = ("x", "zl", "c")
VIEW = ("y", "zh")


def exchange(x, axes):
    return lax.all_to_all(x, axes, 0, 0, tiled=True)


def gather_blocks(x, axes):
    count = lax.axis_size(axes)
    return exchange(jnp.broadcast_to(x[None], (count,) + x.shape), axes)


def sum_blocks(x):
    return jnp.sum(x.astype(F32), axis=0)


def column_order(flip):
    i = lax.broadcasted_iota(jnp.int32, (RT, RT), 0)
    j = lax.broadcasted_iota(jnp.int32, (RT, RT), 1)
    x, zl, c, r = i // 64, (i // 8) % 8, (i // 4) % 2, i % 4
    return ((c ^ flip) * 128 + x * 32 + zl * 4 + r == j).astype(BF16)


def dot(a, b):
    return jnp.dot(a, b, preferred_element_type=F32)


def dot_t(a, b):
    return lax.dot_general(a, b, (((1,), (1,)), ((), ())), preferred_element_type=F32)


def same(shape, left, right):
    return lax.broadcasted_iota(jnp.int32, shape, 0) // left == (
        lax.broadcasted_iota(jnp.int32, shape, 1) // right
    )


SUB = 8
PARAMS = pltpu.CompilerParams(vmem_limit_bytes=24 << 20)
IN_VMEM = pl.BlockSpec(memory_space=pltpu.VMEM)
IN_SMEM = pl.BlockSpec(memory_space=pltpu.SMEM)


def core_band(ref, g):
    nx, ny, nzh = SIZES[0], SIZES[3], SIZES[4]
    near = ref.shape[1] // nzh
    y, z = g // nzh, g % nzh
    return [ref[x * ny + y, z * near : (z + 1) * near, :] for x in range(nx)]


def spread(n):
    return jnp.where(same((n * SUB, n), SUB, 1), 1.0, 0.0).astype(BF16)


def joined(pieces):
    return jnp.concatenate(pieces, axis=1)


def stacked(pieces):
    return jnp.concatenate(pieces, axis=0)


def diagonal(x):
    r = lax.broadcasted_iota(jnp.int32, x.shape, 0) % SUB
    c = lax.broadcasted_iota(jnp.int32, x.shape, 1) % SUB
    return jnp.where(r == c, x, 0.0).astype(BF16)


def copies_kernel(x_ref, out_ref, sems):
    moves = [
        pltpu.make_async_copy(x_ref, out_ref.at[i], sems.at[i]) for i in range(out_ref.shape[0])
    ]
    for move in moves:
        move.start()
    for move in moves:
        move.wait()


def copies(x, count):
    return pl.pallas_call(
        copies_kernel,
        out_shape=jax.ShapeDtypeStruct((count,) + x.shape, x.dtype),
        in_specs=[IN_VMEM],
        out_specs=pl.BlockSpec(memory_space=pl.ANY),
        scratch_shapes=[pltpu.SemaphoreType.DMA((count,))],
        compiler_params=PARAMS,
        cost_estimate=pl.CostEstimate(
            flops=0, bytes_accessed=(count + 1) * x.size * 2, transcendentals=0
        ),
        name="copies",
    )(x)


def first_kernel(
    zh_ref, own_ref, tex_ref, sent_ref, came_ref, high_ref, low_ref,
    part_ref, tall_ref, wide_ref, seen_ref, high_out, low_out,
):
    nzh = SIZES[4]
    rows = part_ref.shape[1]
    groups = rows // SUB
    half = tex_ref.shape[1] // 2
    tex = tex_ref[:, :half]
    for g in range(part_ref.shape[0]):
        part_ref[g] = dot(tex, stacked(core_band(own_ref, g)))

    count = sent_ref.shape[0] // (rows + 1)
    first_half = zh_ref[0] == 0
    sent, came = sent_ref[...].astype(F32), came_ref[...].astype(F32)
    factor, at = [], 0
    for z in range(nzh):
        side = jnp.where(first_half, sent if z == 0 else came, came if z == 0 else sent)
        for lane in range(2):
            lanes = slice(lane * RL, (lane + 1) * RL)
            for i in range(count):
                low = i * rows
                seen_ref[at : at + SUB, :] = joined(
                    [side[low + k * SUB : low + (k + 1) * SUB, lanes] for k in range(groups)]
                )
                at += SUB
            factor.append(side[count * rows :, lanes])
    factor = stacked(factor).astype(BF16)

    spread_v, spread_b = spread(factor.shape[0]), spread(RV)
    tall_ref[...] = diagonal(dot_t(dot(spread_v, factor).astype(BF16), spread_b))
    wide_ref[...] = diagonal(dot_t(dot_t(spread_b, factor).astype(BF16), spread_v))

    for ref, out in ((high_ref, high_out), (low_ref, low_out)):
        gram = ref[...]
        zero = jnp.zeros_like(gram)
        out[...] = stacked(
            [joined([gram if i == k else zero for i in range(groups)]) for k in range(groups)]
        ).astype(BF16)


def keep(x, refs):
    refs[0][...] = x[:, :128]
    rest = x[:, 128:]
    refs[1][...] = joined([rest, jnp.zeros((rest.shape[0], 128 - rest.shape[1]), rest.dtype)])


def second_kernel(
    zh_ref, own_ref, other_ref, part_ref, tall_ref, wide_ref, tex_ref, order_ref, seen_ref,
    high_ref, low_ref, blocks_ref, view_ref, *kept,
):
    ny, nzh = SIZES[3], SIZES[4]
    back_ref, stack_ref = kept[:2], kept[2:]
    bands, rows, width = part_ref.shape
    band = width // RL
    groups = rows // SUB
    half = tex_ref.shape[1] // 2
    tex = tex_ref[:, half:]

    pieces = []
    for g in range(bands):
        p = part_ref[g] + dot(tex, stacked(core_band(other_ref, g)))
        for b in range(band):
            pieces.append(
                joined(
                    [
                        p[k * SUB : (k + 1) * SUB, b * RL : (b + 1) * RL]
                        for k in range(groups)
                    ]
                )
            )
    stack = stacked(pieces)
    keep(stack, stack_ref)
    stack = stack.astype(BF16)
    mixed = dot(tall_ref[...], stack).astype(BF16)
    fitted = dot(mixed, high_ref[...]) + dot(mixed, low_ref[...])
    back = fitted - seen_ref[...]
    keep(back, back_ref)
    back = back.astype(BF16)
    y = dot(wide_ref[...], back)

    first_half = zh_ref[0] == 0
    tex_part, near = None, None
    view_part, views = None, back.shape[0] // SUB
    for g in range(bands):
        y_g = stacked(
            [
                joined(
                    [
                        y[(g * band + b) * SUB : (g * band + b + 1) * SUB, k * RL : (k + 1) * RL]
                        for b in range(band)
                    ]
                )
                for k in range(groups)
            ]
        )
        if g % nzh == 0:
            near = y_g
        else:
            blocks_ref[g // nzh, :, :width] = jnp.where(first_half, near, y_g).astype(BF16)
        core = stacked(core_band(own_ref, g) + core_band(other_ref, g))
        part = dot_t(y_g.astype(BF16), core)
        tex_part = part if tex_part is None else tex_part + part

        for t in range(g, SUB, bands):
            left, right = (
                joined([part[pl.ds(t, n, stride=SUB), :] for part in ref]).astype(BF16)
                for ref, n in ((back_ref, views), (stack_ref, RV))
            )
            part = dot_t(left, right)
            view_part = part if view_part is None else view_part + part

    tex_part = dot_t(tex_part.astype(BF16), order_ref[...]).astype(BF16)
    for i in range(ny):
        blocks_ref[i, :, width:] = tex_part

    height = view_ref.shape[1]
    count = views // nzh
    own = jnp.where(first_half, view_part[:count], view_part[count:])
    own = joined(
        [own[v : v + height, :] for v in range(0, count, height)]
        + [jnp.zeros((height, width - count // height * RL), F32)]
    ).astype(BF16)
    for i in range(view_ref.shape[0]):
        view_ref[i] = own


def cost(flops):
    return pl.CostEstimate(flops=flops, bytes_accessed=flops // 500, transcendentals=0)


def middle(zh, core_own, core_other, tex_rel, order, sent, came, high, low, height):
    rows = tex_rel.shape[0]
    ny, nzh, width = SIZES[3], SIZES[4], core_own.shape[-1]
    views = sent.shape[0] // (rows + 1) * 2 * nzh
    lanes = rows // SUB * RL
    zh = zh.reshape(1)
    part, tall, wide, seen, high, low = pl.pallas_call(
        first_kernel,
        out_shape=(
            jax.ShapeDtypeStruct((ny * nzh, rows, width), F32),
            jax.ShapeDtypeStruct((views * SUB, RV * SUB), BF16),
            jax.ShapeDtypeStruct((RV * SUB, views * SUB), BF16),
            jax.ShapeDtypeStruct((views * SUB, lanes), F32),
            jax.ShapeDtypeStruct((lanes, lanes), BF16),
            jax.ShapeDtypeStruct((lanes, lanes), BF16),
        ),
        in_specs=[IN_SMEM] + [IN_VMEM] * 6,
        out_specs=(IN_VMEM,) * 6,
        compiler_params=PARAMS,
        cost_estimate=cost(10**9),
        name="first",
    )(zh, core_own, tex_rel, sent, came, high, low)
    return pl.pallas_call(
        second_kernel,
        out_shape=(
            jax.ShapeDtypeStruct((ny, rows, width + RT), BF16),
            jax.ShapeDtypeStruct((SIZES[0] * SIZES[2], height, width), BF16),
        ),
        in_specs=[IN_SMEM] + [IN_VMEM] * 10,
        out_specs=(IN_VMEM,) * 2,
        scratch_shapes=[
            pltpu.VMEM((n * SUB, 128), F32) for n in (views, views, RV, RV)
        ],
        compiler_params=PARAMS,
        cost_estimate=cost(2 * 10**9),
        name="second",
    )(zh, core_own, core_other, part, tall, wide, tex_rel, order, seen, high, low)


def last_kernel(
    rates, sums_ref, blocks_ref, tex_ref, view_ref, core_ref, tex_out, view_out, core_out
):
    rate_tex, rate_view, rate_core = rates
    width = sums_ref.shape[-1]
    height = core_ref.shape[0]
    total = jnp.sum(sums_ref[...].astype(F32), axis=0)
    core_grad, view_grad = rate_core * total[:height], rate_view * total[height:]
    for b in range(core_ref.shape[1]):
        core_out[:, b, :] = core_ref[:, b, :] - core_grad[:, b * RL : (b + 1) * RL]
    for b in range(view_ref.shape[0] // height):
        at = slice(b * height, (b + 1) * height)
        view_out[at, :] = view_ref[at, :] - view_grad[:, b * RV : (b + 1) * RV]
    tex_out[...] = tex_ref[...] - rate_tex * blocks_ref[:, width:]


def last(rates, sums, blocks, tex, view, core):
    return pl.pallas_call(
        functools.partial(last_kernel, rates),
        out_shape=tuple(jax.ShapeDtypeStruct(a.shape, F32) for a in (tex, view, core)),
        in_specs=[IN_VMEM] * 5,
        out_specs=(IN_VMEM,) * 3,
        compiler_params=PARAMS,
        cost_estimate=pl.CostEstimate(flops=10**5, bytes_accessed=10**5, transcendentals=0),
        name="last",
    )(sums, blocks, tex, view, core)


def per_device(measured, view_mask, tex_factor, view_factor, light_factor, core_tensor):
    tex_count = lax.axis_size(TEX)
    tex_rows, views = measured.shape[:2]
    core_rows, band = core_tensor.shape[:2]
    width = band * RL
    texels_all = tex_rows * tex_count
    scaling = (RT * RV * RL) ** (-0.5)
    rate_tex = RT / (VALID * L)
    rate_view = RV / (texels_all * L)
    rate_core = RT * RV * RL / (texels_all * VALID * L)
    nx, nzl, nc, ny, nzh = SIZES
    bands = ny * nzh
    near = nzl * core_rows
    zh = lax.axis_index("zh")
    core_bf = core_tensor.astype(BF16).reshape(core_rows, width)

    core_z = gather_blocks(core_bf, ("zh", "zl")).reshape(nzh, near, width)
    weights = view_mask.astype(F32)

    seen = jnp.einsum(
        "vtl,lc->vtc", jnp.transpose(measured, (1, 0, 2)), light_factor, preferred_element_type=F32
    )
    seen = (weights[:, None, None] * seen).astype(BF16)
    masked_bf = (weights[:, None] * view_factor).astype(BF16)
    sent = jnp.concatenate(
        [
            jnp.concatenate([seen[: views // 2], seen[views // 2 :]], axis=2).reshape(-1, 2 * RL),
            jnp.concatenate([masked_bf[: views // 2], masked_bf[views // 2 :]], axis=1),
        ]
    )
    came = lax.ppermute(sent, "zh", [(0, 1), (1, 0)])

    gram = scaling * lax.dot_general(
        light_factor, light_factor, (((0,), (0,)), ((), ())), preferred_element_type=F32
    )
    gram_high = lax.reduce_precision(gram, 8, 7)
    gram_low = gram - gram_high

    core_own = exchange(copies(core_z, nx * ny), ("x", "y")).reshape(nx * ny, nzh * near, width)
    core_other = lax.ppermute(core_own, "c", [(0, 1), (1, 0)])

    tex_raw = tex_factor.astype(BF16)
    order = lax.optimization_barrier(column_order(lax.axis_index("c")))
    tex_rel = dot(tex_raw, order).astype(BF16)
    half = RT // nc
    tex_abs = jnp.where(
        lax.axis_index("c") == 0,
        tex_rel,
        jnp.concatenate([tex_rel[:, half:], tex_rel[:, :half]], axis=1),
    )
    tex_rel, tex_abs = lax.optimization_barrier((tex_rel, tex_abs))

    blocks, view_part = middle(
        zh, core_own, core_other, tex_rel, order, sent, came, gram_high, gram_low, core_rows
    )
    blocks = sum_blocks(exchange(blocks, ("y",)))
    summed = blocks[:, :width].astype(BF16)

    core_part = jnp.einsum("ta,tn->an", tex_abs, summed, preferred_element_type=F32)
    core_part = core_part.astype(BF16).reshape(nx * nc, near, width)
    both = exchange(jnp.concatenate([core_part, view_part], axis=1), ("c", "x"))
    core_part = sum_blocks(both[:, :near]).astype(BF16).reshape(nzl, core_rows, width)
    view_block = sum_blocks(both[:, near:]).astype(BF16)
    view_block = jnp.broadcast_to(view_block[None], (nzl, core_rows, width))
    both = exchange(jnp.concatenate([core_part, view_block], axis=1), ("zl",))
    rates = (scaling * rate_tex, scaling * rate_view, scaling * rate_core)
    return last(rates, both, blocks, tex_factor, view_factor, core_tensor)


def solution(mesh):
    parts = Mesh(mesh.devices.reshape(SIZES), NAMES)
    return jax.shard_map(
        per_device,
        mesh=parts,
        in_specs=(
            P(TEX, VIEW, None),
            P(VIEW),
            P(TEX, None),
            P(VIEW, None),
            P(),
            P(TEX, VIEW, None),
        ),
        out_specs=(P(TEX, None), P(VIEW, None), P(TEX, VIEW, None)),
        check_vma=False,
    )
```

```python
import functools

import jax
import jax.numpy as jnp
from jax import lax
from jax.experimental import pallas as pl
from jax.experimental.pallas import tpu as pltpu
from jax.sharding import Mesh, PartitionSpec as P

RT = 256
RV = 64
RL = 64
VALID = 151
L = 151

F32 = jnp.float32
BF16 = jnp.bfloat16

SIZES = (4, 8, 2, 4, 2)
NAMES = ("x", "zl", "c", "y", "zh")
TEX = ("x", "zl", "c")
VIEW = ("y", "zh")


def exchange(x, axes):
    return lax.all_to_all(x, axes, 0, 0, tiled=True)


def gather_blocks(x, axes):
    count = lax.axis_size(axes)
    return exchange(jnp.broadcast_to(x[None], (count,) + x.shape), axes)


def sum_blocks(x):
    return jnp.sum(x.astype(F32), axis=0)


def column_order(flip):
    i = lax.broadcasted_iota(jnp.int32, (RT, RT), 0)
    j = lax.broadcasted_iota(jnp.int32, (RT, RT), 1)
    x, zl, c, r = i // 64, (i // 8) % 8, (i // 4) % 2, i % 4
    return ((c ^ flip) * 128 + x * 32 + zl * 4 + r == j).astype(BF16)


def dot(a, b):
    return jnp.dot(a, b, preferred_element_type=F32)


def dot_t(a, b):
    return lax.dot_general(a, b, (((1,), (1,)), ((), ())), preferred_element_type=F32)


def same(shape, left, right):
    return lax.broadcasted_iota(jnp.int32, shape, 0) // left == (
        lax.broadcasted_iota(jnp.int32, shape, 1) // right
    )


SUB = 8
PARAMS = pltpu.CompilerParams(vmem_limit_bytes=24 << 20)
IN_VMEM = pl.BlockSpec(memory_space=pltpu.VMEM)
IN_SMEM = pl.BlockSpec(memory_space=pltpu.SMEM)


def core_band(ref, g):
    nx, ny, nzh = SIZES[0], SIZES[3], SIZES[4]
    near = ref.shape[1] // nzh
    y, z = g // nzh, g % nzh
    return [ref[x * ny + y, z * near : (z + 1) * near, :] for x in range(nx)]


def spread(n):
    return jnp.where(same((n * SUB, n), SUB, 1), 1.0, 0.0).astype(BF16)


def joined(pieces):
    return jnp.concatenate(pieces, axis=1)


def stacked(pieces):
    return jnp.concatenate(pieces, axis=0)


def diagonal(x):
    r = lax.broadcasted_iota(jnp.int32, x.shape, 0) % SUB
    c = lax.broadcasted_iota(jnp.int32, x.shape, 1) % SUB
    return jnp.where(r == c, x, 0.0).astype(BF16)


def first_kernel(
    zh_ref, own_ref, tex_ref, sent_ref, came_ref, high_ref, low_ref,
    part_ref, tall_ref, wide_ref, seen_ref, high_out, low_out,
):
    nzh = SIZES[4]
    rows = part_ref.shape[1]
    groups = rows // SUB
    half = tex_ref.shape[1] // 2
    tex = tex_ref[:, :half]
    for g in range(part_ref.shape[0]):
        part_ref[g] = dot(tex, stacked(core_band(own_ref, g)))

    count = sent_ref.shape[0] // (rows + 1)
    first_half = zh_ref[0] == 0
    sent, came = sent_ref[...].astype(F32), came_ref[...].astype(F32)
    factor, at = [], 0
    for z in range(nzh):
        side = jnp.where(first_half, sent if z == 0 else came, came if z == 0 else sent)
        for lane in range(2):
            lanes = slice(lane * RL, (lane + 1) * RL)
            for i in range(count):
                low = i * rows
                seen_ref[at : at + SUB, :] = joined(
                    [side[low + k * SUB : low + (k + 1) * SUB, lanes] for k in range(groups)]
                )
                at += SUB
            factor.append(side[count * rows :, lanes])
    factor = stacked(factor).astype(BF16)

    spread_v, spread_b = spread(factor.shape[0]), spread(RV)
    tall_ref[...] = diagonal(dot_t(dot(spread_v, factor).astype(BF16), spread_b))
    wide_ref[...] = diagonal(dot_t(dot_t(spread_b, factor).astype(BF16), spread_v))

    for ref, out in ((high_ref, high_out), (low_ref, low_out)):
        gram = ref[...]
        zero = jnp.zeros_like(gram)
        out[...] = stacked(
            [joined([gram if i == k else zero for i in range(groups)]) for k in range(groups)]
        ).astype(BF16)


def keep(x, refs):
    refs[0][...] = x[:, :128]
    rest = x[:, 128:]
    refs[1][...] = joined([rest, jnp.zeros((rest.shape[0], 128 - rest.shape[1]), rest.dtype)])


def second_kernel(
    zh_ref, own_ref, other_ref, part_ref, tall_ref, wide_ref, tex_ref, order_ref, seen_ref,
    high_ref, low_ref, blocks_ref, view_ref, *kept,
):
    ny, nzh = SIZES[3], SIZES[4]
    back_ref, stack_ref = kept[:2], kept[2:]
    bands, rows, width = part_ref.shape
    band = width // RL
    groups = rows // SUB
    half = tex_ref.shape[1] // 2
    tex = tex_ref[:, half:]

    pieces = []
    for g in range(bands):
        p = part_ref[g] + dot(tex, stacked(core_band(other_ref, g)))
        for b in range(band):
            pieces.append(
                joined(
                    [
                        p[k * SUB : (k + 1) * SUB, b * RL : (b + 1) * RL]
                        for k in range(groups)
                    ]
                )
            )
    stack = stacked(pieces)
    keep(stack, stack_ref)
    stack = stack.astype(BF16)
    mixed = dot(tall_ref[...], stack).astype(BF16)
    fitted = dot(mixed, high_ref[...]) + dot(mixed, low_ref[...])
    back = fitted - seen_ref[...]
    keep(back, back_ref)
    back = back.astype(BF16)
    y = dot(wide_ref[...], back)

    first_half = zh_ref[0] == 0
    tex_part, near = None, None
    view_part, views = None, back.shape[0] // SUB
    for g in range(bands):
        y_g = stacked(
            [
                joined(
                    [
                        y[(g * band + b) * SUB : (g * band + b + 1) * SUB, k * RL : (k + 1) * RL]
                        for b in range(band)
                    ]
                )
                for k in range(groups)
            ]
        )
        if g % nzh == 0:
            near = y_g
        else:
            blocks_ref[g // nzh, :, :width] = jnp.where(first_half, near, y_g).astype(BF16)
        core = stacked(core_band(own_ref, g) + core_band(other_ref, g))
        part = dot_t(y_g.astype(BF16), core)
        tex_part = part if tex_part is None else tex_part + part

        for t in range(g, SUB, bands):
            left, right = (
                joined([part[pl.ds(t, n, stride=SUB), :] for part in ref]).astype(BF16)
                for ref, n in ((back_ref, views), (stack_ref, RV))
            )
            part = dot_t(left, right)
            view_part = part if view_part is None else view_part + part

    tex_part = dot_t(tex_part.astype(BF16), order_ref[...]).astype(BF16)
    for i in range(ny):
        blocks_ref[i, :, width:] = tex_part

    height = view_ref.shape[1]
    count = views // nzh
    own = jnp.where(first_half, view_part[:count], view_part[count:])
    own = joined(
        [own[v : v + height, :] for v in range(0, count, height)]
        + [jnp.zeros((height, width - count // height * RL), F32)]
    ).astype(BF16)
    for i in range(view_ref.shape[0]):
        view_ref[i] = own


def cost(flops):
    return pl.CostEstimate(flops=flops, bytes_accessed=flops // 500, transcendentals=0)


def middle(zh, core_own, core_other, tex_rel, order, sent, came, high, low, height):
    rows = tex_rel.shape[0]
    ny, nzh, width = SIZES[3], SIZES[4], core_own.shape[-1]
    views = sent.shape[0] // (rows + 1) * 2 * nzh
    lanes = rows // SUB * RL
    zh = zh.reshape(1)
    part, tall, wide, seen, high, low = pl.pallas_call(
        first_kernel,
        out_shape=(
            jax.ShapeDtypeStruct((ny * nzh, rows, width), F32),
            jax.ShapeDtypeStruct((views * SUB, RV * SUB), BF16),
            jax.ShapeDtypeStruct((RV * SUB, views * SUB), BF16),
            jax.ShapeDtypeStruct((views * SUB, lanes), F32),
            jax.ShapeDtypeStruct((lanes, lanes), BF16),
            jax.ShapeDtypeStruct((lanes, lanes), BF16),
        ),
        in_specs=[IN_SMEM] + [IN_VMEM] * 6,
        out_specs=(IN_VMEM,) * 6,
        compiler_params=PARAMS,
        cost_estimate=cost(10**9),
        name="first",
    )(zh, core_own, tex_rel, sent, came, high, low)
    return pl.pallas_call(
        second_kernel,
        out_shape=(
            jax.ShapeDtypeStruct((ny, rows, width + RT), BF16),
            jax.ShapeDtypeStruct((SIZES[0] * SIZES[2], height, width), BF16),
        ),
        in_specs=[IN_SMEM] + [IN_VMEM] * 10,
        out_specs=(IN_VMEM,) * 2,
        scratch_shapes=[
            pltpu.VMEM((n * SUB, 128), F32) for n in (views, views, RV, RV)
        ],
        compiler_params=PARAMS,
        cost_estimate=cost(2 * 10**9),
        name="second",
    )(zh, core_own, core_other, part, tall, wide, tex_rel, order, seen, high, low)


def last_kernel(
    rates, sums_ref, blocks_ref, tex_ref, view_ref, core_ref, tex_out, view_out, core_out
):
    rate_tex, rate_view, rate_core = rates
    width = sums_ref.shape[-1]
    height = core_ref.shape[0]
    total = jnp.sum(sums_ref[...].astype(F32), axis=0)
    core_grad, view_grad = rate_core * total[:height], rate_view * total[height:]
    for b in range(core_ref.shape[1]):
        core_out[:, b, :] = core_ref[:, b, :] - core_grad[:, b * RL : (b + 1) * RL]
    for b in range(view_ref.shape[0] // height):
        at = slice(b * height, (b + 1) * height)
        view_out[at, :] = view_ref[at, :] - view_grad[:, b * RV : (b + 1) * RV]
    tex_out[...] = tex_ref[...] - rate_tex * blocks_ref[:, width:]


def last(rates, sums, blocks, tex, view, core):
    return pl.pallas_call(
        functools.partial(last_kernel, rates),
        out_shape=tuple(jax.ShapeDtypeStruct(a.shape, F32) for a in (tex, view, core)),
        in_specs=[IN_VMEM] * 5,
        out_specs=(IN_VMEM,) * 3,
        compiler_params=PARAMS,
        cost_estimate=pl.CostEstimate(flops=10**5, bytes_accessed=10**5, transcendentals=0),
        name="last",
    )(sums, blocks, tex, view, core)


def per_device(measured, view_mask, tex_factor, view_factor, light_factor, core_tensor):
    tex_count = lax.axis_size(TEX)
    tex_rows, views = measured.shape[:2]
    core_rows, band = core_tensor.shape[:2]
    width = band * RL
    texels_all = tex_rows * tex_count
    scaling = (RT * RV * RL) ** (-0.5)
    rate_tex = RT / (VALID * L)
    rate_view = RV / (texels_all * L)
    rate_core = RT * RV * RL / (texels_all * VALID * L)
    nx, nzl, nc, ny, nzh = SIZES
    bands = ny * nzh
    near = nzl * core_rows
    zh = lax.axis_index("zh")
    core_bf = core_tensor.astype(BF16).reshape(core_rows, width)

    core_z = gather_blocks(core_bf, ("zh", "zl")).reshape(nzh, near, width)
    weights = view_mask.astype(F32)

    seen = jnp.einsum(
        "vtl,lc->vtc", jnp.transpose(measured, (1, 0, 2)), light_factor, preferred_element_type=F32
    )
    seen = (weights[:, None, None] * seen).astype(BF16)
    masked_bf = (weights[:, None] * view_factor).astype(BF16)
    sent = jnp.concatenate(
        [
            jnp.concatenate([seen[: views // 2], seen[views // 2 :]], axis=2).reshape(-1, 2 * RL),
            jnp.concatenate([masked_bf[: views // 2], masked_bf[views // 2 :]], axis=1),
        ]
    )
    came = lax.ppermute(sent, "zh", [(0, 1), (1, 0)])

    gram = scaling * lax.dot_general(
        light_factor, light_factor, (((0,), (0,)), ((), ())), preferred_element_type=F32
    )
    gram_high = lax.reduce_precision(gram, 8, 7)
    gram_low = gram - gram_high

    core_own = gather_blocks(core_z, ("x", "y")).reshape(nx * ny, nzh * near, width)
    core_other = lax.ppermute(core_own, "c", [(0, 1), (1, 0)])

    tex_raw = tex_factor.astype(BF16)
    order = lax.optimization_barrier(column_order(lax.axis_index("c")))
    tex_rel = dot(tex_raw, order).astype(BF16)
    half = RT // nc
    tex_abs = jnp.where(
        lax.axis_index("c") == 0,
        tex_rel,
        jnp.concatenate([tex_rel[:, half:], tex_rel[:, :half]], axis=1),
    )
    tex_rel, tex_abs = lax.optimization_barrier((tex_rel, tex_abs))

    blocks, view_part = middle(
        zh, core_own, core_other, tex_rel, order, sent, came, gram_high, gram_low, core_rows
    )
    blocks = sum_blocks(exchange(blocks, ("y",)))
    summed = blocks[:, :width].astype(BF16)

    core_part = jnp.einsum("ta,tn->an", tex_abs, summed, preferred_element_type=F32)
    core_part = core_part.astype(BF16).reshape(nc, nx, near, width)
    core_part = jnp.transpose(core_part, (1, 0, 2, 3)).reshape(nx * nc, near, width)
    both = exchange(jnp.concatenate([core_part, view_part], axis=1), ("x", "c"))
    core_part = sum_blocks(both[:, :near]).astype(BF16).reshape(nzl, core_rows, width)
    view_block = sum_blocks(both[:, near:]).astype(BF16)
    view_block = jnp.broadcast_to(view_block[None], (nzl, core_rows, width))
    both = exchange(jnp.concatenate([core_part, view_block], axis=1), ("zl",))
    rates = (scaling * rate_tex, scaling * rate_view, scaling * rate_core)
    return last(rates, both, blocks, tex_factor, view_factor, core_tensor)


def solution(mesh):
    parts = Mesh(mesh.devices.reshape(SIZES), NAMES)
    return jax.shard_map(
        per_device,
        mesh=parts,
        in_specs=(
            P(TEX, VIEW, None),
            P(VIEW),
            P(TEX, None),
            P(VIEW, None),
            P(),
            P(TEX, VIEW, None),
        ),
        out_specs=(P(TEX, None), P(VIEW, None), P(TEX, VIEW, None)),
        check_vma=False,
    )
```

```python
import functools

import jax
import jax.numpy as jnp
from jax import lax
from jax.experimental import pallas as pl
from jax.experimental.pallas import tpu as pltpu
from jax.sharding import Mesh, PartitionSpec as P

RT = 256
RV = 64
RL = 64
VALID = 151
L = 151

F32 = jnp.float32
BF16 = jnp.bfloat16

SIZES = (4, 8, 2, 4, 2)
NAMES = ("x", "zl", "c", "y", "zh")
TEX = ("x", "zl", "c")
VIEW = ("y", "zh")


def exchange(x, axes):
    return lax.all_to_all(x, axes, 0, 0, tiled=True)


def gather_blocks(x, axes):
    count = lax.axis_size(axes)
    return exchange(jnp.broadcast_to(x[None], (count,) + x.shape), axes)


def sum_blocks(x):
    return jnp.sum(x.astype(F32), axis=0)


def column_order(flip):
    i = lax.broadcasted_iota(jnp.int32, (RT, RT), 0)
    j = lax.broadcasted_iota(jnp.int32, (RT, RT), 1)
    x, zl, c, r = i // 64, (i // 8) % 8, (i // 4) % 2, i % 4
    return ((c ^ flip) * 128 + x * 32 + zl * 4 + r == j).astype(BF16)


def dot(a, b):
    return jnp.dot(a, b, preferred_element_type=F32)


def dot_t(a, b):
    return lax.dot_general(a, b, (((1,), (1,)), ((), ())), preferred_element_type=F32)


def same(shape, left, right):
    return lax.broadcasted_iota(jnp.int32, shape, 0) // left == (
        lax.broadcasted_iota(jnp.int32, shape, 1) // right
    )


SUB = 8
PARAMS = pltpu.CompilerParams(vmem_limit_bytes=24 << 20)
IN_VMEM = pl.BlockSpec(memory_space=pltpu.VMEM)
IN_SMEM = pl.BlockSpec(memory_space=pltpu.SMEM)


def core_band(ref, g):
    nx, nzh = SIZES[0], SIZES[4]
    near = ref.shape[1] // nzh
    y, z = g // nzh, g % nzh
    return [ref[y * nx + x, z * near : (z + 1) * near, :] for x in range(nx)]


def spread(n):
    return jnp.where(same((n * SUB, n), SUB, 1), 1.0, 0.0).astype(BF16)


def joined(pieces):
    return jnp.concatenate(pieces, axis=1)


def stacked(pieces):
    return jnp.concatenate(pieces, axis=0)


def diagonal(x):
    r = lax.broadcasted_iota(jnp.int32, x.shape, 0) % SUB
    c = lax.broadcasted_iota(jnp.int32, x.shape, 1) % SUB
    return jnp.where(r == c, x, 0.0).astype(BF16)


def first_kernel(
    zh_ref, own_ref, tex_ref, sent_ref, came_ref, high_ref, low_ref,
    part_ref, tall_ref, wide_ref, seen_ref, high_out, low_out,
):
    nzh = SIZES[4]
    rows = part_ref.shape[1]
    groups = rows // SUB
    half = tex_ref.shape[1] // 2
    tex = tex_ref[:, :half]
    for g in range(part_ref.shape[0]):
        part_ref[g] = dot(tex, stacked(core_band(own_ref, g)))

    count = sent_ref.shape[0] // (rows + 1)
    first_half = zh_ref[0] == 0
    sent, came = sent_ref[...].astype(F32), came_ref[...].astype(F32)
    factor, at = [], 0
    for z in range(nzh):
        side = jnp.where(first_half, sent if z == 0 else came, came if z == 0 else sent)
        for lane in range(2):
            lanes = slice(lane * RL, (lane + 1) * RL)
            for i in range(count):
                low = i * rows
                seen_ref[at : at + SUB, :] = joined(
                    [side[low + k * SUB : low + (k + 1) * SUB, lanes] for k in range(groups)]
                )
                at += SUB
            factor.append(side[count * rows :, lanes])
    factor = stacked(factor).astype(BF16)

    spread_v, spread_b = spread(factor.shape[0]), spread(RV)
    tall_ref[...] = diagonal(dot_t(dot(spread_v, factor).astype(BF16), spread_b))
    wide_ref[...] = diagonal(dot_t(dot_t(spread_b, factor).astype(BF16), spread_v))

    for ref, out in ((high_ref, high_out), (low_ref, low_out)):
        gram = ref[...]
        zero = jnp.zeros_like(gram)
        out[...] = stacked(
            [joined([gram if i == k else zero for i in range(groups)]) for k in range(groups)]
        ).astype(BF16)


def keep(x, refs):
    refs[0][...] = x[:, :128]
    rest = x[:, 128:]
    refs[1][...] = joined([rest, jnp.zeros((rest.shape[0], 128 - rest.shape[1]), rest.dtype)])


def second_kernel(
    zh_ref, own_ref, other_ref, part_ref, tall_ref, wide_ref, tex_ref, order_ref, seen_ref,
    high_ref, low_ref, blocks_ref, view_ref, *kept,
):
    ny, nzh = SIZES[3], SIZES[4]
    back_ref, stack_ref = kept[:2], kept[2:]
    bands, rows, width = part_ref.shape
    band = width // RL
    groups = rows // SUB
    half = tex_ref.shape[1] // 2
    tex = tex_ref[:, half:]

    pieces = []
    for g in range(bands):
        p = part_ref[g] + dot(tex, stacked(core_band(other_ref, g)))
        for b in range(band):
            pieces.append(
                joined(
                    [
                        p[k * SUB : (k + 1) * SUB, b * RL : (b + 1) * RL]
                        for k in range(groups)
                    ]
                )
            )
    stack = stacked(pieces)
    keep(stack, stack_ref)
    stack = stack.astype(BF16)
    mixed = dot(tall_ref[...], stack).astype(BF16)
    fitted = dot(mixed, high_ref[...]) + dot(mixed, low_ref[...])
    back = fitted - seen_ref[...]
    keep(back, back_ref)
    back = back.astype(BF16)
    y = dot(wide_ref[...], back)

    first_half = zh_ref[0] == 0
    tex_part, near = None, None
    view_part, views = None, back.shape[0] // SUB
    for g in range(bands):
        y_g = stacked(
            [
                joined(
                    [
                        y[(g * band + b) * SUB : (g * band + b + 1) * SUB, k * RL : (k + 1) * RL]
                        for b in range(band)
                    ]
                )
                for k in range(groups)
            ]
        )
        if g % nzh == 0:
            near = y_g
        else:
            blocks_ref[g // nzh, :, :width] = jnp.where(first_half, near, y_g).astype(BF16)
        core = stacked(core_band(own_ref, g) + core_band(other_ref, g))
        part = dot_t(y_g.astype(BF16), core)
        tex_part = part if tex_part is None else tex_part + part

        for t in range(g, SUB, bands):
            left, right = (
                joined([part[pl.ds(t, n, stride=SUB), :] for part in ref]).astype(BF16)
                for ref, n in ((back_ref, views), (stack_ref, RV))
            )
            part = dot_t(left, right)
            view_part = part if view_part is None else view_part + part

    tex_part = dot_t(tex_part.astype(BF16), order_ref[...]).astype(BF16)
    for i in range(ny):
        blocks_ref[i, :, width:] = tex_part

    height = view_ref.shape[1]
    count = views // nzh
    own = jnp.where(first_half, view_part[:count], view_part[count:])
    own = joined(
        [own[v : v + height, :] for v in range(0, count, height)]
        + [jnp.zeros((height, width - count // height * RL), F32)]
    ).astype(BF16)
    for i in range(view_ref.shape[0]):
        view_ref[i] = own


def cost(flops):
    return pl.CostEstimate(flops=flops, bytes_accessed=flops // 500, transcendentals=0)


def middle(zh, core_own, core_other, tex_rel, order, sent, came, high, low, height):
    rows = tex_rel.shape[0]
    ny, nzh, width = SIZES[3], SIZES[4], core_own.shape[-1]
    views = sent.shape[0] // (rows + 1) * 2 * nzh
    lanes = rows // SUB * RL
    zh = zh.reshape(1)
    part, tall, wide, seen, high, low = pl.pallas_call(
        first_kernel,
        out_shape=(
            jax.ShapeDtypeStruct((ny * nzh, rows, width), F32),
            jax.ShapeDtypeStruct((views * SUB, RV * SUB), BF16),
            jax.ShapeDtypeStruct((RV * SUB, views * SUB), BF16),
            jax.ShapeDtypeStruct((views * SUB, lanes), F32),
            jax.ShapeDtypeStruct((lanes, lanes), BF16),
            jax.ShapeDtypeStruct((lanes, lanes), BF16),
        ),
        in_specs=[IN_SMEM] + [IN_VMEM] * 6,
        out_specs=(IN_VMEM,) * 6,
        compiler_params=PARAMS,
        cost_estimate=cost(10**9),
        name="first",
    )(zh, core_own, tex_rel, sent, came, high, low)
    return pl.pallas_call(
        second_kernel,
        out_shape=(
            jax.ShapeDtypeStruct((ny, rows, width + RT), BF16),
            jax.ShapeDtypeStruct((SIZES[0] * SIZES[2], height, width), BF16),
        ),
        in_specs=[IN_SMEM] + [IN_VMEM] * 10,
        out_specs=(IN_VMEM,) * 2,
        scratch_shapes=[
            pltpu.VMEM((n * SUB, 128), F32) for n in (views, views, RV, RV)
        ],
        compiler_params=PARAMS,
        cost_estimate=cost(2 * 10**9),
        name="second",
    )(zh, core_own, core_other, part, tall, wide, tex_rel, order, seen, high, low)


def last_kernel(
    rates, sums_ref, blocks_ref, tex_ref, view_ref, core_ref, tex_out, view_out, core_out
):
    rate_tex, rate_view, rate_core = rates
    width = sums_ref.shape[-1]
    height = core_ref.shape[0]
    total = jnp.sum(sums_ref[...].astype(F32), axis=0)
    core_grad, view_grad = rate_core * total[:height], rate_view * total[height:]
    for b in range(core_ref.shape[1]):
        core_out[:, b, :] = core_ref[:, b, :] - core_grad[:, b * RL : (b + 1) * RL]
    for b in range(view_ref.shape[0] // height):
        at = slice(b * height, (b + 1) * height)
        view_out[at, :] = view_ref[at, :] - view_grad[:, b * RV : (b + 1) * RV]
    tex_out[...] = tex_ref[...] - rate_tex * blocks_ref[:, width:]


def last(rates, sums, blocks, tex, view, core):
    return pl.pallas_call(
        functools.partial(last_kernel, rates),
        out_shape=tuple(jax.ShapeDtypeStruct(a.shape, F32) for a in (tex, view, core)),
        in_specs=[IN_VMEM] * 5,
        out_specs=(IN_VMEM,) * 3,
        compiler_params=PARAMS,
        cost_estimate=pl.CostEstimate(flops=10**5, bytes_accessed=10**5, transcendentals=0),
        name="last",
    )(sums, blocks, tex, view, core)


def per_device(measured, view_mask, tex_factor, view_factor, light_factor, core_tensor):
    tex_count = lax.axis_size(TEX)
    tex_rows, views = measured.shape[:2]
    core_rows, band = core_tensor.shape[:2]
    width = band * RL
    texels_all = tex_rows * tex_count
    scaling = (RT * RV * RL) ** (-0.5)
    rate_tex = RT / (VALID * L)
    rate_view = RV / (texels_all * L)
    rate_core = RT * RV * RL / (texels_all * VALID * L)
    nx, nzl, nc, ny, nzh = SIZES
    bands = ny * nzh
    near = nzl * core_rows
    zh = lax.axis_index("zh")
    core_bf = core_tensor.astype(BF16).reshape(core_rows, width)

    core_z = gather_blocks(core_bf, ("zh", "zl")).reshape(nzh, near, width)
    weights = view_mask.astype(F32)

    seen = jnp.einsum(
        "vtl,lc->vtc", jnp.transpose(measured, (1, 0, 2)), light_factor, preferred_element_type=F32
    )
    seen = (weights[:, None, None] * seen).astype(BF16)
    masked_bf = (weights[:, None] * view_factor).astype(BF16)
    sent = jnp.concatenate(
        [
            jnp.concatenate([seen[: views // 2], seen[views // 2 :]], axis=2).reshape(-1, 2 * RL),
            jnp.concatenate([masked_bf[: views // 2], masked_bf[views // 2 :]], axis=1),
        ]
    )
    came = lax.ppermute(sent, "zh", [(0, 1), (1, 0)])

    gram = scaling * lax.dot_general(
        light_factor, light_factor, (((0,), (0,)), ((), ())), preferred_element_type=F32
    )
    gram_high = lax.reduce_precision(gram, 8, 7)
    gram_low = gram - gram_high

    core_own = gather_blocks(core_z, ("y", "x")).reshape(nx * ny, nzh * near, width)
    core_other = lax.ppermute(core_own, "c", [(0, 1), (1, 0)])

    tex_raw = tex_factor.astype(BF16)
    order = lax.optimization_barrier(column_order(lax.axis_index("c")))
    tex_rel = dot(tex_raw, order).astype(BF16)
    half = RT // nc
    tex_abs = jnp.where(
        lax.axis_index("c") == 0,
        tex_rel,
        jnp.concatenate([tex_rel[:, half:], tex_rel[:, :half]], axis=1),
    )
    tex_rel, tex_abs = lax.optimization_barrier((tex_rel, tex_abs))

    blocks, view_part = middle(
        zh, core_own, core_other, tex_rel, order, sent, came, gram_high, gram_low, core_rows
    )
    blocks = sum_blocks(exchange(blocks, ("y",)))
    summed = blocks[:, :width].astype(BF16)

    core_part = jnp.einsum("ta,tn->an", tex_abs, summed, preferred_element_type=F32)
    core_part = core_part.astype(BF16).reshape(nc, nx, near, width)
    core_part = jnp.transpose(core_part, (1, 0, 2, 3)).reshape(nx * nc, near, width)
    both = exchange(jnp.concatenate([core_part, view_part], axis=1), ("x", "c"))
    core_part = sum_blocks(both[:, :near]).astype(BF16).reshape(nzl, core_rows, width)
    view_block = sum_blocks(both[:, near:]).astype(BF16)
    view_block = jnp.broadcast_to(view_block[None], (nzl, core_rows, width))
    both = exchange(jnp.concatenate([core_part, view_block], axis=1), ("zl",))
    rates = (scaling * rate_tex, scaling * rate_view, scaling * rate_core)
    return last(rates, both, blocks, tex_factor, view_factor, core_tensor)


def solution(mesh):
    parts = Mesh(mesh.devices.reshape(SIZES), NAMES)
    return jax.shard_map(
        per_device,
        mesh=parts,
        in_specs=(
            P(TEX, VIEW, None),
            P(VIEW),
            P(TEX, None),
            P(VIEW, None),
            P(),
            P(TEX, VIEW, None),
        ),
        out_specs=(P(TEX, None), P(VIEW, None), P(TEX, VIEW, None)),
        check_vma=False,
    )
```

```python
import functools

import jax
import jax.numpy as jnp
from jax import lax
from jax.experimental import pallas as pl
from jax.experimental.pallas import tpu as pltpu
from jax.sharding import Mesh, PartitionSpec as P

RT = 256
RV = 64
RL = 64
VALID = 151
L = 151

F32 = jnp.float32
BF16 = jnp.bfloat16

SIZES = (4, 8, 2, 4, 2)
NAMES = ("x", "zl", "c", "y", "zh")
TEX = ("x", "zl", "c")
VIEW = ("y", "zh")


def exchange(x, axes):
    return lax.all_to_all(x, axes, 0, 0, tiled=True)


def gather_blocks(x, axes):
    count = lax.axis_size(axes)
    return exchange(jnp.broadcast_to(x[None], (count,) + x.shape), axes)


def sum_blocks(x):
    return jnp.sum(x.astype(F32), axis=0)


def column_order(flip):
    i = lax.broadcasted_iota(jnp.int32, (RT, RT), 0)
    j = lax.broadcasted_iota(jnp.int32, (RT, RT), 1)
    x, zl, c, r = i // 64, (i // 8) % 8, (i // 4) % 2, i % 4
    return ((c ^ flip) * 128 + x * 32 + zl * 4 + r == j).astype(BF16)


def dot(a, b):
    return jnp.dot(a, b, preferred_element_type=F32)


def dot_t(a, b):
    return lax.dot_general(a, b, (((1,), (1,)), ((), ())), preferred_element_type=F32)


def same(shape, left, right):
    return lax.broadcasted_iota(jnp.int32, shape, 0) // left == (
        lax.broadcasted_iota(jnp.int32, shape, 1) // right
    )


SUB = 8
PARAMS = pltpu.CompilerParams(vmem_limit_bytes=24 << 20)
IN_VMEM = pl.BlockSpec(memory_space=pltpu.VMEM)
IN_SMEM = pl.BlockSpec(memory_space=pltpu.SMEM)


def core_band(ref, g):
    nx, ny, nzh = SIZES[0], SIZES[3], SIZES[4]
    near = ref.shape[1] // nzh
    y, z = g // nzh, g % nzh
    return [ref[x * ny + y, z * near : (z + 1) * near, :] for x in range(nx)]


def spread(n):
    return jnp.where(same((n * SUB, n), SUB, 1), 1.0, 0.0).astype(BF16)


def joined(pieces):
    return jnp.concatenate(pieces, axis=1)


def stacked(pieces):
    return jnp.concatenate(pieces, axis=0)


def diagonal(x):
    r = lax.broadcasted_iota(jnp.int32, x.shape, 0) % SUB
    c = lax.broadcasted_iota(jnp.int32, x.shape, 1) % SUB
    return jnp.where(r == c, x, 0.0).astype(BF16)


def first_kernel(
    zh_ref, own_ref, tex_ref, sent_ref, came_ref, high_ref, low_ref,
    part_ref, tall_ref, wide_ref, seen_ref, high_out, low_out,
):
    nzh = SIZES[4]
    rows = part_ref.shape[1]
    groups = rows // SUB
    half = tex_ref.shape[1] // 2
    tex = tex_ref[:, :half]
    for g in range(part_ref.shape[0]):
        part_ref[g] = dot(tex, stacked(core_band(own_ref, g)))

    count = sent_ref.shape[0] // (rows + 1)
    first_half = zh_ref[0] == 0
    sent, came = sent_ref[...].astype(F32), came_ref[...].astype(F32)
    factor, at = [], 0
    for z in range(nzh):
        side = jnp.where(first_half, sent if z == 0 else came, came if z == 0 else sent)
        for lane in range(2):
            lanes = slice(lane * RL, (lane + 1) * RL)
            for i in range(count):
                low = i * rows
                seen_ref[at : at + SUB, :] = joined(
                    [side[low + k * SUB : low + (k + 1) * SUB, lanes] for k in range(groups)]
                )
                at += SUB
            factor.append(side[count * rows :, lanes])
    factor = stacked(factor).astype(BF16)

    spread_v, spread_b = spread(factor.shape[0]), spread(RV)
    tall_ref[...] = diagonal(dot_t(dot(spread_v, factor).astype(BF16), spread_b))
    wide_ref[...] = diagonal(dot_t(dot_t(spread_b, factor).astype(BF16), spread_v))

    for ref, out in ((high_ref, high_out), (low_ref, low_out)):
        gram = ref[...]
        zero = jnp.zeros_like(gram)
        out[...] = stacked(
            [joined([gram if i == k else zero for i in range(groups)]) for k in range(groups)]
        ).astype(BF16)


def keep(x, refs):
    refs[0][...] = x[:, :128]
    rest = x[:, 128:]
    refs[1][...] = joined([rest, jnp.zeros((rest.shape[0], 128 - rest.shape[1]), rest.dtype)])


def second_kernel(
    zh_ref, own_ref, other_ref, part_ref, tall_ref, wide_ref, tex_ref, order_ref, seen_ref,
    high_ref, low_ref, blocks_ref, view_ref, *kept,
):
    ny, nzh = SIZES[3], SIZES[4]
    back_ref, stack_ref = kept[:2], kept[2:]
    bands, rows, width = part_ref.shape
    band = width // RL
    groups = rows // SUB
    half = tex_ref.shape[1] // 2
    tex = tex_ref[:, half:]

    pieces = []
    for g in range(bands):
        p = part_ref[g] + dot(tex, stacked(core_band(other_ref, g)))
        for b in range(band):
            pieces.append(
                joined(
                    [
                        p[k * SUB : (k + 1) * SUB, b * RL : (b + 1) * RL]
                        for k in range(groups)
                    ]
                )
            )
    stack = stacked(pieces)
    keep(stack, stack_ref)
    stack = stack.astype(BF16)
    mixed = dot(tall_ref[...], stack).astype(BF16)
    fitted = dot(mixed, high_ref[...]) + dot(mixed, low_ref[...])
    back = fitted - seen_ref[...]
    keep(back, back_ref)
    back = back.astype(BF16)
    y = dot(wide_ref[...], back)

    first_half = zh_ref[0] == 0
    tex_part, near = None, None
    view_part, views = None, back.shape[0] // SUB
    for g in range(bands):
        y_g = stacked(
            [
                joined(
                    [
                        y[(g * band + b) * SUB : (g * band + b + 1) * SUB, k * RL : (k + 1) * RL]
                        for b in range(band)
                    ]
                )
                for k in range(groups)
            ]
        )
        if g % nzh == 0:
            near = y_g
        else:
            blocks_ref[g // nzh, :, :width] = jnp.where(first_half, near, y_g).astype(BF16)
        core = stacked(core_band(own_ref, g) + core_band(other_ref, g))
        part = dot_t(y_g.astype(BF16), core)
        tex_part = part if tex_part is None else tex_part + part

        for t in range(g, SUB, bands):
            left, right = (
                joined([part[pl.ds(t, n, stride=SUB), :] for part in ref]).astype(BF16)
                for ref, n in ((back_ref, views), (stack_ref, RV))
            )
            part = dot_t(left, right)
            view_part = part if view_part is None else view_part + part

    tex_part = dot_t(tex_part.astype(BF16), order_ref[...]).astype(BF16)
    for i in range(ny):
        blocks_ref[i, :, width:] = tex_part

    height = view_ref.shape[1]
    count = views // nzh
    own = jnp.where(first_half, view_part[:count], view_part[count:])
    own = joined(
        [own[v : v + height, :] for v in range(0, count, height)]
        + [jnp.zeros((height, width - count // height * RL), F32)]
    ).astype(BF16)
    for i in range(view_ref.shape[0]):
        view_ref[i] = own


def cost(flops):
    return pl.CostEstimate(flops=flops, bytes_accessed=flops // 500, transcendentals=0)


def middle(zh, core_own, core_other, tex_rel, order, sent, came, high, low, height):
    rows = tex_rel.shape[0]
    ny, nzh, width = SIZES[3], SIZES[4], core_own.shape[-1]
    views = sent.shape[0] // (rows + 1) * 2 * nzh
    lanes = rows // SUB * RL
    zh = zh.reshape(1)
    part, tall, wide, seen, high, low = pl.pallas_call(
        first_kernel,
        out_shape=(
            jax.ShapeDtypeStruct((ny * nzh, rows, width), F32),
            jax.ShapeDtypeStruct((views * SUB, RV * SUB), BF16),
            jax.ShapeDtypeStruct((RV * SUB, views * SUB), BF16),
            jax.ShapeDtypeStruct((views * SUB, lanes), F32),
            jax.ShapeDtypeStruct((lanes, lanes), BF16),
            jax.ShapeDtypeStruct((lanes, lanes), BF16),
        ),
        in_specs=[IN_SMEM] + [IN_VMEM] * 6,
        out_specs=(IN_VMEM,) * 6,
        compiler_params=PARAMS,
        cost_estimate=cost(10**9),
        name="first",
    )(zh, core_own, tex_rel, sent, came, high, low)
    return pl.pallas_call(
        second_kernel,
        out_shape=(
            jax.ShapeDtypeStruct((ny, rows, width + RT), BF16),
            jax.ShapeDtypeStruct((SIZES[0] * SIZES[2], height, width), BF16),
        ),
        in_specs=[IN_SMEM] + [IN_VMEM] * 10,
        out_specs=(IN_VMEM,) * 2,
        scratch_shapes=[
            pltpu.VMEM((n * SUB, 128), F32) for n in (views, views, RV, RV)
        ],
        compiler_params=pltpu.CompilerParams(
            vmem_limit_bytes=24 << 20
        ),
        cost_estimate=cost(2 * 10**9),
        name="second",
    )(zh, core_own, core_other, part, tall, wide, tex_rel, order, seen, high, low)


def last_kernel(
    rates, sums_ref, blocks_ref, tex_ref, view_ref, core_ref, tex_out, view_out, core_out
):
    rate_tex, rate_view, rate_core = rates
    width = sums_ref.shape[-1]
    height = core_ref.shape[0]
    total = jnp.sum(sums_ref[...].astype(F32), axis=0)
    core_grad, view_grad = rate_core * total[:height], rate_view * total[height:]
    for b in range(core_ref.shape[1]):
        core_out[:, b, :] = core_ref[:, b, :] - core_grad[:, b * RL : (b + 1) * RL]
    for b in range(view_ref.shape[0] // height):
        at = slice(b * height, (b + 1) * height)
        view_out[at, :] = view_ref[at, :] - view_grad[:, b * RV : (b + 1) * RV]
    tex_out[...] = tex_ref[...] - rate_tex * blocks_ref[:, width:]


def last(rates, sums, blocks, tex, view, core):
    return pl.pallas_call(
        functools.partial(last_kernel, rates),
        out_shape=tuple(jax.ShapeDtypeStruct(a.shape, F32) for a in (tex, view, core)),
        in_specs=[IN_VMEM] * 5,
        out_specs=(IN_VMEM,) * 3,
        compiler_params=PARAMS,
        cost_estimate=pl.CostEstimate(flops=10**5, bytes_accessed=10**5, transcendentals=0),
        name="last",
    )(sums, blocks, tex, view, core)


def per_device(measured, view_mask, tex_factor, view_factor, light_factor, core_tensor):
    tex_count = lax.axis_size(TEX)
    tex_rows, views = measured.shape[:2]
    core_rows, band = core_tensor.shape[:2]
    width = band * RL
    texels_all = tex_rows * tex_count
    scaling = (RT * RV * RL) ** (-0.5)
    rate_tex = RT / (VALID * L)
    rate_view = RV / (texels_all * L)
    rate_core = RT * RV * RL / (texels_all * VALID * L)
    nx, nzl, nc, ny, nzh = SIZES
    bands = ny * nzh
    near = nzl * core_rows
    zh = lax.axis_index("zh")
    core_bf = core_tensor.astype(BF16).reshape(core_rows, width)

    core_z = gather_blocks(core_bf, ("zh", "zl")).reshape(nzh, near, width)
    weights = view_mask.astype(F32)

    seen = jnp.einsum(
        "vtl,lc->vtc", jnp.transpose(measured, (1, 0, 2)), light_factor, preferred_element_type=F32
    )
    seen = (weights[:, None, None] * seen).astype(BF16)
    masked_bf = (weights[:, None] * view_factor).astype(BF16)
    sent = jnp.concatenate(
        [
            jnp.concatenate([seen[: views // 2], seen[views // 2 :]], axis=2).reshape(-1, 2 * RL),
            jnp.concatenate([masked_bf[: views // 2], masked_bf[views // 2 :]], axis=1),
        ]
    )
    came = lax.ppermute(sent, "zh", [(0, 1), (1, 0)])

    gram = scaling * lax.dot_general(
        light_factor, light_factor, (((0,), (0,)), ((), ())), preferred_element_type=F32
    )
    gram_high = lax.reduce_precision(gram, 8, 7)
    gram_low = gram - gram_high

    core_own = gather_blocks(core_z, ("x", "y")).reshape(nx * ny, nzh * near, width)
    core_other = lax.ppermute(core_own, "c", [(0, 1), (1, 0)])

    tex_raw = tex_factor.astype(BF16)
    order = lax.optimization_barrier(column_order(lax.axis_index("c")))
    tex_rel = dot(tex_raw, order).astype(BF16)
    half = RT // nc
    tex_abs = jnp.where(
        lax.axis_index("c") == 0,
        tex_rel,
        jnp.concatenate([tex_rel[:, half:], tex_rel[:, :half]], axis=1),
    )
    tex_rel, tex_abs = lax.optimization_barrier((tex_rel, tex_abs))

    blocks, view_part = middle(
        zh, core_own, core_other, tex_rel, order, sent, came, gram_high, gram_low, core_rows
    )
    blocks = sum_blocks(exchange(blocks, ("y",)))
    summed = blocks[:, :width].astype(BF16)

    core_part = jnp.einsum("ta,tn->an", tex_abs, summed, preferred_element_type=F32)
    core_part = core_part.astype(BF16).reshape(nc, nx, near, width)
    core_part = jnp.transpose(core_part, (1, 0, 2, 3)).reshape(nx * nc, near, width)
    both = exchange(jnp.concatenate([core_part, view_part], axis=1), ("x", "c"))
    core_part = sum_blocks(both[:, :near]).astype(BF16).reshape(nzl, core_rows, width)
    view_block = sum_blocks(both[:, near:]).astype(BF16)
    view_block = jnp.broadcast_to(view_block[None], (nzl, core_rows, width))
    both = exchange(jnp.concatenate([core_part, view_block], axis=1), ("zl",))
    rates = (scaling * rate_tex, scaling * rate_view, scaling * rate_core)
    return last(rates, both, blocks, tex_factor, view_factor, core_tensor)


def solution(mesh):
    parts = Mesh(mesh.devices.reshape(SIZES), NAMES)
    return jax.shard_map(
        per_device,
        mesh=parts,
        in_specs=(
            P(TEX, VIEW, None),
            P(VIEW),
            P(TEX, None),
            P(VIEW, None),
            P(),
            P(TEX, VIEW, None),
        ),
        out_specs=(P(TEX, None), P(VIEW, None), P(TEX, VIEW, None)),
        check_vma=False,
    )
```

```python
import functools

import jax
import jax.numpy as jnp
from jax import lax
from jax.experimental import pallas as pl
from jax.experimental.pallas import tpu as pltpu
from jax.sharding import Mesh, PartitionSpec as P

RT = 256
RV = 64
RL = 64
VALID = 151
L = 151

F32 = jnp.float32
BF16 = jnp.bfloat16

SIZES = (4, 8, 2, 4, 2)
NAMES = ("x", "zl", "c", "y", "zh")
TEX = ("x", "zl", "c")
VIEW = ("y", "zh")


def exchange(x, axes):
    return lax.all_to_all(x, axes, 0, 0, tiled=True)


def gather_blocks(x, axes):
    count = lax.axis_size(axes)
    return exchange(jnp.broadcast_to(x[None], (count,) + x.shape), axes)


def sum_blocks(x):
    return jnp.sum(x.astype(F32), axis=0)


def column_order(flip):
    i = lax.broadcasted_iota(jnp.int32, (RT, RT), 0)
    j = lax.broadcasted_iota(jnp.int32, (RT, RT), 1)
    x, zl, c, r = i // 64, (i // 8) % 8, (i // 4) % 2, i % 4
    return ((c ^ flip) * 128 + x * 32 + zl * 4 + r == j).astype(BF16)


def dot(a, b):
    return jnp.dot(a, b, preferred_element_type=F32)


def dot_t(a, b):
    return lax.dot_general(a, b, (((1,), (1,)), ((), ())), preferred_element_type=F32)


def same(shape, left, right):
    return lax.broadcasted_iota(jnp.int32, shape, 0) // left == (
        lax.broadcasted_iota(jnp.int32, shape, 1) // right
    )


SUB = 8
PARAMS = pltpu.CompilerParams(vmem_limit_bytes=24 << 20)
IN_VMEM = pl.BlockSpec(memory_space=pltpu.VMEM)
IN_SMEM = pl.BlockSpec(memory_space=pltpu.SMEM)


def core_band(ref, g):
    nx, ny, nzh = SIZES[0], SIZES[3], SIZES[4]
    near = ref.shape[1] // nzh
    y, z = g // nzh, g % nzh
    return [ref[x * ny + y, z * near : (z + 1) * near, :] for x in range(nx)]


def spread(n):
    return jnp.where(same((n * SUB, n), SUB, 1), 1.0, 0.0).astype(BF16)


def joined(pieces):
    return jnp.concatenate(pieces, axis=1)


def stacked(pieces):
    return jnp.concatenate(pieces, axis=0)


def diagonal(x):
    r = lax.broadcasted_iota(jnp.int32, x.shape, 0) % SUB
    c = lax.broadcasted_iota(jnp.int32, x.shape, 1) % SUB
    return jnp.where(r == c, x, 0.0).astype(BF16)


def first_kernel(
    zh_ref, own_ref, tex_ref, sent_ref, came_ref, high_ref, low_ref,
    part_ref, tall_ref, wide_ref, seen_ref, high_out, low_out,
):
    nzh = SIZES[4]
    rows = part_ref.shape[1]
    groups = rows // SUB
    half = tex_ref.shape[1] // 2
    tex = tex_ref[:, :half]
    for g in range(part_ref.shape[0]):
        part_ref[g] = dot(tex, stacked(core_band(own_ref, g)))

    count = sent_ref.shape[0] // (rows + 1)
    first_half = zh_ref[0] == 0
    sent, came = sent_ref[...].astype(F32), came_ref[...].astype(F32)
    factor, at = [], 0
    for z in range(nzh):
        side = jnp.where(first_half, sent if z == 0 else came, came if z == 0 else sent)
        for lane in range(2):
            lanes = slice(lane * RL, (lane + 1) * RL)
            for i in range(count):
                low = i * rows
                seen_ref[at : at + SUB, :] = joined(
                    [side[low + k * SUB : low + (k + 1) * SUB, lanes] for k in range(groups)]
                )
                at += SUB
            factor.append(side[count * rows :, lanes])
    factor = stacked(factor).astype(BF16)

    spread_v, spread_b = spread(factor.shape[0]), spread(RV)
    tall_ref[...] = diagonal(dot_t(dot(spread_v, factor).astype(BF16), spread_b))
    wide_ref[...] = diagonal(dot_t(dot_t(spread_b, factor).astype(BF16), spread_v))

    for ref, out in ((high_ref, high_out), (low_ref, low_out)):
        gram = ref[...]
        zero = jnp.zeros_like(gram)
        out[...] = stacked(
            [joined([gram if i == k else zero for i in range(groups)]) for k in range(groups)]
        ).astype(BF16)


def keep(x, refs):
    refs[0][...] = x[:, :128]
    rest = x[:, 128:]
    refs[1][...] = joined([rest, jnp.zeros((rest.shape[0], 128 - rest.shape[1]), rest.dtype)])


def second_kernel(
    zh_ref, own_ref, other_ref, part_ref, tall_ref, wide_ref, tex_ref, order_ref, seen_ref,
    high_ref, low_ref, blocks_ref, view_ref, *kept,
):
    ny, nzh = SIZES[3], SIZES[4]
    back_ref, stack_ref = kept[:2], kept[2:]
    bands, rows, width = part_ref.shape
    band = width // RL
    groups = rows // SUB
    half = tex_ref.shape[1] // 2
    tex = tex_ref[:, half:]

    pieces = []
    for g in range(bands):
        p = part_ref[g] + dot(tex, stacked(core_band(other_ref, g)))
        for b in range(band):
            pieces.append(
                joined(
                    [
                        p[k * SUB : (k + 1) * SUB, b * RL : (b + 1) * RL]
                        for k in range(groups)
                    ]
                )
            )
    stack = stacked(pieces)
    keep(stack, stack_ref)
    stack = stack.astype(BF16)
    mixed = dot(tall_ref[...], stack).astype(BF16)
    fitted = dot(mixed, high_ref[...]) + dot(mixed, low_ref[...])
    back = fitted - seen_ref[...]
    keep(back, back_ref)
    back = back.astype(BF16)
    y = dot(wide_ref[...], back)

    first_half = zh_ref[0] == 0
    tex_part, near = None, None
    view_part, views = None, back.shape[0] // SUB
    for g in range(bands):
        y_g = stacked(
            [
                joined(
                    [
                        y[(g * band + b) * SUB : (g * band + b + 1) * SUB, k * RL : (k + 1) * RL]
                        for b in range(band)
                    ]
                )
                for k in range(groups)
            ]
        )
        if g % nzh == 0:
            near = y_g
        else:
            blocks_ref[g // nzh, :, :width] = jnp.where(first_half, near, y_g).astype(BF16)
        core = stacked(core_band(own_ref, g) + core_band(other_ref, g))
        part = dot_t(y_g.astype(BF16), core)
        tex_part = part if tex_part is None else tex_part + part

        for t in range(g, SUB, bands):
            left, right = (
                joined([part[pl.ds(t, n, stride=SUB), :] for part in ref]).astype(BF16)
                for ref, n in ((back_ref, views), (stack_ref, RV))
            )
            part = dot_t(left, right)
            view_part = part if view_part is None else view_part + part

    tex_part = dot_t(tex_part.astype(BF16), order_ref[...]).astype(BF16)
    for i in range(ny):
        blocks_ref[i, :, width:] = tex_part

    height = view_ref.shape[1]
    count = views // nzh
    own = jnp.where(first_half, view_part[:count], view_part[count:])
    own = joined(
        [own[v : v + height, :] for v in range(0, count, height)]
        + [jnp.zeros((height, width - count // height * RL), F32)]
    ).astype(BF16)
    for i in range(view_ref.shape[0]):
        view_ref[i] = own


def cost(flops):
    return pl.CostEstimate(flops=flops, bytes_accessed=flops // 500, transcendentals=0)


def middle(zh, core_own, core_other, tex_rel, order, sent, came, high, low, height):
    rows = tex_rel.shape[0]
    ny, nzh, width = SIZES[3], SIZES[4], core_own.shape[-1]
    views = sent.shape[0] // (rows + 1) * 2 * nzh
    lanes = rows // SUB * RL
    zh = zh.reshape(1)
    part, tall, wide, seen, high, low = pl.pallas_call(
        first_kernel,
        out_shape=(
            jax.ShapeDtypeStruct((ny * nzh, rows, width), F32),
            jax.ShapeDtypeStruct((views * SUB, RV * SUB), BF16),
            jax.ShapeDtypeStruct((RV * SUB, views * SUB), BF16),
            jax.ShapeDtypeStruct((views * SUB, lanes), F32),
            jax.ShapeDtypeStruct((lanes, lanes), BF16),
            jax.ShapeDtypeStruct((lanes, lanes), BF16),
        ),
        in_specs=[IN_SMEM] + [IN_VMEM] * 6,
        out_specs=(IN_VMEM,) * 6,
        compiler_params=PARAMS,
        cost_estimate=cost(10**9),
        name="first",
    )(zh, core_own, tex_rel, sent, came, high, low)
    return pl.pallas_call(
        second_kernel,
        out_shape=(
            jax.ShapeDtypeStruct((ny, rows, width + RT), BF16),
            jax.ShapeDtypeStruct((SIZES[0] * SIZES[2], height, width), BF16),
        ),
        in_specs=[IN_SMEM] + [IN_VMEM] * 10,
        out_specs=(IN_VMEM,) * 2,
        scratch_shapes=[
            pltpu.VMEM((n * SUB, 128), F32) for n in (views, views, RV, RV)
        ],
        compiler_params=PARAMS,
        cost_estimate=cost(2 * 10**9),
        name="second",
    )(zh, core_own, core_other, part, tall, wide, tex_rel, order, seen, high, low)


def last_kernel(
    rates, sums_ref, blocks_ref, tex_ref, view_ref, core_ref, tex_out, view_out, core_out
):
    rate_tex, rate_view, rate_core = rates
    width = sums_ref.shape[-1]
    height = core_ref.shape[0]
    total = jnp.sum(sums_ref[...].astype(F32), axis=0)
    core_grad, view_grad = rate_core * total[:height], rate_view * total[height:]
    for b in range(core_ref.shape[1]):
        core_out[:, b, :] = core_ref[:, b, :] - core_grad[:, b * RL : (b + 1) * RL]
    for b in range(view_ref.shape[0] // height):
        at = slice(b * height, (b + 1) * height)
        view_out[at, :] = view_ref[at, :] - view_grad[:, b * RV : (b + 1) * RV]
    tex_out[...] = tex_ref[...] - rate_tex * blocks_ref[:, width:]


def last(rates, sums, blocks, tex, view, core):
    return pl.pallas_call(
        functools.partial(last_kernel, rates),
        out_shape=tuple(jax.ShapeDtypeStruct(a.shape, F32) for a in (tex, view, core)),
        in_specs=[IN_VMEM] * 5,
        out_specs=(IN_VMEM,) * 3,
        compiler_params=PARAMS,
        cost_estimate=pl.CostEstimate(flops=10**5, bytes_accessed=10**5, transcendentals=0),
        name="last",
    )(sums, blocks, tex, view, core)


def per_device(measured, view_mask, tex_factor, view_factor, light_factor, core_tensor):
    tex_count = lax.axis_size(TEX)
    tex_rows, views = measured.shape[:2]
    core_rows, band = core_tensor.shape[:2]
    width = band * RL
    texels_all = tex_rows * tex_count
    scaling = (RT * RV * RL) ** (-0.5)
    rate_tex = RT / (VALID * L)
    rate_view = RV / (texels_all * L)
    rate_core = RT * RV * RL / (texels_all * VALID * L)
    nx, nzl, nc, ny, nzh = SIZES
    bands = ny * nzh
    near = nzl * core_rows
    zh = lax.axis_index("zh")
    core_bf = core_tensor.astype(BF16).reshape(core_rows, width)

    core_z = gather_blocks(core_bf, ("zh", "zl")).reshape(nzh, near, width)
    weights = view_mask.astype(F32)

    seen = jnp.einsum(
        "vtl,lc->vtc", jnp.transpose(measured, (1, 0, 2)), light_factor, preferred_element_type=F32
    )
    seen = (weights[:, None, None] * seen).astype(BF16)
    masked_bf = (weights[:, None] * view_factor).astype(BF16)
    sent = jnp.concatenate(
        [
            jnp.concatenate([seen[: views // 2], seen[views // 2 :]], axis=2).reshape(-1, 2 * RL),
            jnp.concatenate([masked_bf[: views // 2], masked_bf[views // 2 :]], axis=1),
        ]
    )
    came = lax.ppermute(sent, "zh", [(0, 1), (1, 0)])

    gram = scaling * lax.dot_general(
        light_factor, light_factor, (((0,), (0,)), ((), ())), preferred_element_type=F32
    )
    gram_high = lax.reduce_precision(gram, 8, 7)
    gram_low = gram - gram_high

    core_own = gather_blocks(core_z, ("x", "y")).reshape(nx * ny, nzh * near, width)

    tex_raw = tex_factor.astype(BF16)
    order = lax.optimization_barrier(column_order(lax.axis_index("c")))
    tex_rel = dot(tex_raw, order).astype(BF16)
    half = RT // nc
    tex_abs = jnp.where(
        lax.axis_index("c") == 0,
        tex_rel,
        jnp.concatenate([tex_rel[:, half:], tex_rel[:, :half]], axis=1),
    )
    core_own, order, tex_rel, tex_abs, gram_high, gram_low = lax.optimization_barrier(
        (core_own, order, tex_rel, tex_abs, gram_high, gram_low)
    )
    core_other = lax.ppermute(core_own, "c", [(0, 1), (1, 0)])

    blocks, view_part = middle(
        zh, core_own, core_other, tex_rel, order, sent, came, gram_high, gram_low, core_rows
    )
    blocks = sum_blocks(exchange(blocks, ("y",)))
    summed = blocks[:, :width].astype(BF16)

    core_part = jnp.einsum("ta,tn->an", tex_abs, summed, preferred_element_type=F32)
    core_part = core_part.astype(BF16).reshape(nc, nx, near, width)
    core_part = jnp.transpose(core_part, (1, 0, 2, 3)).reshape(nx * nc, near, width)
    both = exchange(jnp.concatenate([core_part, view_part], axis=1), ("x", "c"))
    core_part = sum_blocks(both[:, :near]).astype(BF16).reshape(nzl, core_rows, width)
    view_block = sum_blocks(both[:, near:]).astype(BF16)
    view_block = jnp.broadcast_to(view_block[None], (nzl, core_rows, width))
    both = exchange(jnp.concatenate([core_part, view_block], axis=1), ("zl",))
    rates = (scaling * rate_tex, scaling * rate_view, scaling * rate_core)
    return last(rates, both, blocks, tex_factor, view_factor, core_tensor)


def solution(mesh):
    parts = Mesh(mesh.devices.reshape(SIZES), NAMES)
    return jax.shard_map(
        per_device,
        mesh=parts,
        in_specs=(
            P(TEX, VIEW, None),
            P(VIEW),
            P(TEX, None),
            P(VIEW, None),
            P(),
            P(TEX, VIEW, None),
        ),
        out_specs=(P(TEX, None), P(VIEW, None), P(TEX, VIEW, None)),
        check_vma=False,
    )
```
